32 devices in a mesh: tile: 8 (over z, x), wave: 4 (over y, core).
Axes of the slice: x: 2, y: 2, z: 4, core: 2. Of those that a mesh axis runs over, the one named last changes fastest.
Arguments:
- fibre_data: bfloat16 [128, 256, 128], P('wave', 'tile'), may hold values from -162 to 162
- kernels: bfloat16 [4, 256, 4, 128, 128], P('wave', 'tile'), may hold values from -0.25 to 0.25
- block_index: int32 [4, 256, 4], P('wave', 'tile'), may hold values from 0 to 127, as said below
- live_count: int32 [8], P('tile'), may hold values from 8 to 32, as said below
Outputs:
- solution: float32 [128, 128, 128], P('wave', 'tile')
- residual: float32 [128, 128, 128], P('wave', 'tile')
The draws below stay inside these ranges and needn't reach their ends.
Inputs may be any that keep to these rules, and one draw needn't show every extreme that they name: `block_index`: A group of tile t (groups t * 32 to (t + 1) * 32 - 1) names only blocks from max(t * 16 - 4, 0) to min((t + 1) * 16 + 4, 128) - 1; for every kernel set and tile, some live group of that tile names both ends of that range. `live_count`: some tile has all 32 groups live.
All inputs are finite; a program needn't handle non-finite values.
Results may differ from the reference program's by a relative error of at most 0.035.
Values may be sent and summed in bfloat16 or wider, within the bound.
No kernel may reach another device: no remote copies, remote signals or barrier semaphores. Data moves between devices by JAX's collectives and lax.ppermute only.
A program may use at most 64 MiB of HBM per device.

```python
import jax
import jax.numpy as jnp
from jax import lax

SLAB_WAVES = 128
KERNEL_WAVES = 32
KERNEL_SETS = 4
SPAXELS = 128
FIBRES = 128
BLOCK_SLOTS = 4
HALO_BLOCKS = 4
BLOCKS_DEV = 16
ITERATIONS = 3
GROUPS_DEV = 32
TILE_COUNT = 8
BLOCKS_ALL = 128
GROUPS_ALL = 256


def draw_block_index(key, part):
    keys = jax.random.split(jax.random.fold_in(key, 11), 5)
    shape = (KERNEL_SETS, GROUPS_ALL, BLOCK_SLOTS)
    group_ids = jnp.arange(GROUPS_ALL, dtype=jnp.int32)[None, :, None]
    tile_ids = group_ids // GROUPS_DEV
    centre = tile_ids * BLOCKS_DEV + jax.random.randint(keys[0], shape, 0, BLOCKS_DEV)
    shifted = centre + jax.random.randint(keys[1], shape, -HALO_BLOCKS, HALO_BLOCKS + 1)
    lowest = jnp.maximum(tile_ids * BLOCKS_DEV - HALO_BLOCKS, 0)
    highest = jnp.minimum((tile_ids + 1) * BLOCKS_DEV + HALO_BLOCKS - 1, BLOCKS_ALL - 1)
    shifted = jnp.clip(shifted, lowest, highest)
    chosen = jax.random.randint(keys[2], (KERNEL_SETS, TILE_COUNT), 0, max(1, GROUPS_DEV // 4))
    slot_low = jax.random.randint(keys[3], (KERNEL_SETS, TILE_COUNT), 0, BLOCK_SLOTS)
    slot_high = (slot_low + 1 + jax.random.randint(keys[4], (KERNEL_SETS, TILE_COUNT), 0, BLOCK_SLOTS - 1)) % BLOCK_SLOTS
    tile_flat = jnp.arange(GROUPS_ALL, dtype=jnp.int32) // GROUPS_DEV
    chosen_group = jnp.take(chosen, tile_flat, axis=1)[:, :, None]
    low_slot = jnp.take(slot_low, tile_flat, axis=1)[:, :, None]
    high_slot = jnp.take(slot_high, tile_flat, axis=1)[:, :, None]
    slot_ids = jnp.arange(BLOCK_SLOTS, dtype=jnp.int32)[None, None, :]
    is_chosen = group_ids % GROUPS_DEV == chosen_group
    shifted = jnp.where(is_chosen & (slot_ids == low_slot), lowest, shifted)
    shifted = jnp.where(is_chosen & (slot_ids == high_slot), highest, shifted)
    return shifted.astype(jnp.int32)


def draw_live_count(key, part):
    keys = jax.random.split(jax.random.fold_in(key, 23), 2)
    counts = jax.random.randint(keys[0], (TILE_COUNT,), max(1, GROUPS_DEV // 4), GROUPS_DEV + 1)
    full_tile = jax.random.randint(keys[1], (), 0, TILE_COUNT)
    counts = jnp.where(jnp.arange(TILE_COUNT, dtype=jnp.int32) == full_tile, GROUPS_DEV, counts)
    return counts.astype(jnp.int32)


def draw_fibre_data(key, part):
    keys = jax.random.split(jax.random.fold_in(key, 37), 3)
    shape = (SLAB_WAVES, GROUPS_ALL, FIBRES)
    group_tile = (jnp.arange(GROUPS_ALL, dtype=jnp.int32) // GROUPS_DEV).astype(jnp.float32)
    position = group_tile / max(TILE_COUNT - 1, 1)
    fibre_scale = jnp.exp(jax.random.uniform(keys[0], (1, GROUPS_ALL, FIBRES), jnp.float32, jnp.log(0.3), jnp.log(3.0)))
    wave_scale = jnp.exp(jax.random.uniform(keys[1], (SLAB_WAVES, 1, 1), jnp.float32, jnp.log(0.3), jnp.log(3.0)))
    ramp = jnp.exp(jnp.log(3.0) * position)
    noise = jnp.clip(jax.random.normal(keys[2], shape, jnp.float32), -4.0, 4.0)
    values = 0.5 * noise * fibre_scale * wave_scale * ramp[None, :, None]
    return values.astype(jnp.bfloat16)


def steps_of(stream_key, shape, shards, smallest, high):
    level, own = 1.0, jax.random.fold_in(stream_key, 6)
    for dim, parts in shards:
        heights = jnp.exp(jax.random.uniform(jax.random.fold_in(own, dim), (parts,), jnp.float32, smallest / len(shards), high / len(shards)))
        level = level * jnp.repeat(heights, shape[dim] // parts).reshape([-1 if axis == dim else 1 for axis in range(len(shape))])
    return level


def scatter_about(stream_key, shape, scale, bound, cuts=(), held_as=jnp.bfloat16):
    factor_of = steps_of(stream_key, shape, cuts, -0.22, 0.18) if cuts else 1.0
    array = jax.random.normal(stream_key, shape, jnp.float32) * scale * factor_of
    return jnp.minimum(jnp.maximum(array, -bound), bound).astype(held_as)


def setup_inputs(seed: int = 0) -> dict:
    key_list = jax.random.split(jax.random.key(seed), 5)
    fibre_data = draw_fibre_data(jax.random.fold_in(key_list[4], 71), 0)
    kernels = scatter_about(key_list[1], (KERNEL_SETS, GROUPS_ALL, BLOCK_SLOTS, SPAXELS, FIBRES), (BLOCK_SLOTS * SPAXELS) ** -0.5, 0.25, ((0, 4), (1, 8)))
    block_index = draw_block_index(jax.random.fold_in(key_list[4], 71), 0)
    live_count = draw_live_count(jax.random.fold_in(key_list[4], 71), 0)
    return dict(fibre_data=fibre_data, kernels=kernels, block_index=block_index, live_count=live_count)


TIKHONOV = 0.5


def select_table(local_index, extent):
    return (local_index[..., None] == jnp.arange(extent, dtype=jnp.int32)).astype(jnp.float32)


def forward_image(window16, kernel_tile, selector16, live_mask):
    kernel_sets = kernel_tile.shape[0]
    shaped = window16.reshape(kernel_sets, window16.shape[0] // kernel_sets, window16.shape[1], window16.shape[2])
    picked = jnp.einsum("cgrb,cwbs->cwgrs", selector16.astype(jnp.float32), shaped.astype(jnp.float32), precision=lax.Precision.HIGHEST).astype(jnp.bfloat16)
    applied = jnp.einsum("cwgrs,cgrsf->cwgf", picked.astype(jnp.float32), kernel_tile.astype(jnp.float32), precision=lax.Precision.HIGHEST)
    return (applied * live_mask[None, None, :, None]).astype(jnp.bfloat16)


def adjoint_image(image16, kernel_tile, selector):
    spread = jnp.einsum("cwgf,cgrsf->cwgrs", image16.astype(jnp.float32), kernel_tile.astype(jnp.float32), precision=lax.Precision.HIGHEST)
    summed = jnp.einsum("cgrb,cwgrs->cwbs", selector, spread, precision=lax.Precision.HIGHEST)
    return summed.reshape(summed.shape[0] * summed.shape[1], summed.shape[2], summed.shape[3])


def reference(fibre_data, kernels, block_index, live_count):
    extent = BLOCKS_DEV + 2 * HALO_BLOCKS
    kernel_sets = kernels.shape[0]
    tile_ids = jnp.arange(TILE_COUNT, dtype=jnp.int32)

    def tile_pieces(tile):
        group_first = tile * GROUPS_DEV
        kernel_tile = lax.dynamic_slice_in_dim(kernels, group_first, GROUPS_DEV, 1)
        index_tile = lax.dynamic_slice_in_dim(block_index, group_first, GROUPS_DEV, 1) - (tile * BLOCKS_DEV - HALO_BLOCKS)
        selector = select_table(index_tile.astype(jnp.int32), extent)
        live_mask = (jnp.arange(GROUPS_DEV, dtype=jnp.int32) < live_count[tile]).astype(jnp.float32)
        return kernel_tile, selector, live_mask

    def accumulate(total, tile, partial_value):
        start = (tile * BLOCKS_DEV).astype(jnp.int32)
        window = lax.dynamic_slice_in_dim(total, start, extent, 1)
        return lax.dynamic_update_slice_in_dim(total, window + partial_value, start, 1)

    empty = jnp.zeros((SLAB_WAVES, BLOCKS_ALL + 2 * HALO_BLOCKS, SPAXELS), jnp.float32)

    def rhs_step(total, tile):
        kernel_tile, selector, live_mask = tile_pieces(tile)
        data_tile = lax.dynamic_slice_in_dim(fibre_data, tile * GROUPS_DEV, GROUPS_DEV, 1)
        observed = data_tile * live_mask.astype(jnp.bfloat16)[None, :, None]
        observed = observed.reshape(kernel_sets, KERNEL_WAVES, GROUPS_DEV, FIBRES)
        return accumulate(total, tile, adjoint_image(observed, kernel_tile, selector)), None

    rhs_padded, _ = lax.scan(rhs_step, empty, tile_ids)
    rhs = rhs_padded[:, HALO_BLOCKS:HALO_BLOCKS + BLOCKS_ALL]

    def operate(vector):
        padded = jnp.pad(vector.astype(jnp.bfloat16), ((0, 0), (HALO_BLOCKS, HALO_BLOCKS), (0, 0)))

        def apply_step(total, tile):
            kernel_tile, selector, live_mask = tile_pieces(tile)
            window = lax.dynamic_slice_in_dim(padded, tile * BLOCKS_DEV, extent, 1)
            image16 = forward_image(window, kernel_tile, selector.astype(jnp.bfloat16), live_mask)
            return accumulate(total, tile, adjoint_image(image16, kernel_tile, selector)), None

        total, _ = lax.scan(apply_step, empty, tile_ids)
        return total[:, HALO_BLOCKS:HALO_BLOCKS + BLOCKS_ALL] + TIKHONOV * vector

    solution = jnp.zeros_like(rhs)
    residual = rhs
    direction = rhs
    current = jnp.sum(residual * residual)
    for iteration in range(ITERATIONS):
        applied = operate(direction)
        step_size = current / jnp.sum(direction * applied)
        solution = solution + step_size * direction
        residual = residual - step_size * applied
        following = jnp.sum(residual * residual)
        direction = residual + (following / current) * direction
        current = following
    return solution, residual
```

```python
import functools

import jax
import jax.numpy as jnp
from jax import lax
from jax.experimental import pallas as pl
from jax.experimental.pallas import tpu as pltpu
from jax.sharding import PartitionSpec as P

HALO_BLOCKS = 4
BLOCKS_DEV = 16
EXTENT = BLOCKS_DEV + 2 * HALO_BLOCKS
RIM = 2 * HALO_BLOCKS
TIKHONOV = 0.5
UNROLL = 4
MOMENT_ROWS = 8
VMEM_LIMIT = 24 * 1024 * 1024


def split(value):
    upper = value.astype(jnp.bfloat16)
    lower = (value - upper.astype(jnp.float32)).astype(jnp.bfloat16)
    return upper, lower


def halves_sum(value):
    half = value.shape[0] // 2
    return value[:half] + value[half:]


def row_of(value):
    total = jnp.sum(value, axis=0, keepdims=True)
    return total if total.ndim == 2 else jnp.sum(total, axis=1)


def scatter(spread, index_ref, group, slots, partial_ref):
    lanes = partial_ref.shape[2]
    for slot in range(slots):
        block = index_ref[group * slots + slot]
        partial_ref[block] += spread[:, slot * lanes : (slot + 1) * lanes]


def emit_rims(place_ref, partial_ref, even_ref, odd_ref):
    width = even_ref.shape[0]
    top = EXTENT - width
    is_even = lax.rem(place_ref[0], 2) == 0
    even_ref[...] = partial_ref[pl.ds(jnp.where(is_even, top, 0), width)]
    odd_ref[...] = partial_ref[pl.ds(jnp.where(is_even, 0, top), width)]


def rhs_kernel(place_ref, index_ref, data_ref, kernels_ref, partial_ref, even_ref, odd_ref):
    groups, slots, spaxels, fibres = kernels_ref.shape
    partial_ref[...] = jnp.zeros_like(partial_ref)
    live = place_ref[1]

    def body(step, carry):
        for inner in range(UNROLL):
            group = step * UNROLL + inner
            weights = kernels_ref[group].reshape(slots * spaxels, fibres)
            data = data_ref[group]
            data = jnp.where(group < live, data, jnp.zeros_like(data))
            spread = lax.dot_general(
                data, weights, (((1,), (1,)), ((), ())), preferred_element_type=jnp.float32
            )
            scatter(spread, index_ref, group, slots, partial_ref)
        return carry

    lax.fori_loop(0, groups // UNROLL, body, 0)
    emit_rims(place_ref, partial_ref, even_ref, odd_ref)


def step_kernel(
    power,
    final,
    place_ref,
    index_ref,
    held_ref,
    even_in_ref,
    odd_in_ref,
    moments_in_ref,
    kernels_ref,
    vector_ref,
    partial_ref,
    even_ref,
    odd_ref,
    moments_ref,
    operand_ref,
):
    groups, slots, spaxels, fibres = kernels_ref.shape
    waves = held_ref.shape[1]
    live = place_ref[1]
    is_even = lax.rem(place_ref[0], 2) == 0
    top = EXTENT - RIM
    vector_ref[...] = held_ref[...]
    vector_ref[pl.ds(jnp.where(is_even, top, 0), RIM)] += even_in_ref[...]
    vector_ref[pl.ds(jnp.where(is_even, 0, top), RIM)] += odd_in_ref[...]
    square = jnp.zeros(vector_ref.shape[1:], jnp.float32)
    for block in range(EXTENT):
        value = vector_ref[block]
        operand_ref[block, :waves], operand_ref[block, waves:] = split(value)
        if HALO_BLOCKS <= block < HALO_BLOCKS + BLOCKS_DEV:
            square = square + value * value
    partial_ref[...] = jnp.zeros_like(partial_ref)

    def body(step, energy):
        for inner in range(UNROLL):
            group = step * UNROLL + inner
            weights = kernels_ref[group].reshape(slots * spaxels, fibres)
            picked = jnp.concatenate(
                [operand_ref[index_ref[group * slots + slot]] for slot in range(slots)], axis=1
            )
            image = halves_sum(jnp.dot(picked, weights, preferred_element_type=jnp.float32))
            image = jnp.where(group < live, image, 0.0)
            energy = energy + image * image
            spread = lax.dot_general(
                jnp.concatenate(split(image), axis=0),
                weights,
                (((1,), (1,)), ((), ())),
                preferred_element_type=jnp.float32,
            )
            scatter(halves_sum(spread), index_ref, group, slots, partial_ref)
        return energy

    energy = lax.fori_loop(
        0, groups // UNROLL, body, jnp.zeros((waves, fibres), jnp.float32)
    )
    emit_rims(place_ref, partial_ref, even_ref, odd_ref)
    for block in range(EXTENT):
        partial_ref[block] += TIKHONOV * vector_ref[block]
    square_row = jnp.sum(square, axis=0, keepdims=True)
    energy_row = jnp.sum(energy, axis=0, keepdims=True) + TIKHONOV * square_row
    rows = lax.broadcasted_iota(jnp.int32, moments_in_ref.shape, 0)
    moments = jnp.where(
        rows == 2 * power,
        square_row,
        jnp.where(rows == 2 * power + 1, energy_row, moments_in_ref[...]),
    )
    moments_ref[...] = jnp.broadcast_to(moments, moments_ref.shape) if final else moments


def coefficients(moments, steps):
    def inner(first, second, shift):
        total = 0.0
        for i, a in enumerate(first):
            for j, b in enumerate(second):
                if a is not None and b is not None:
                    total = total + a * b * moments[i + j + shift]
        return total

    one = jnp.ones_like(moments[0])
    residual, direction = [one], [one]
    answer = []
    current = inner(residual, residual, 0)
    for step in range(steps):
        size = current / inner(direction, direction, 1)
        answer = [
            size * d + (answer[i] if i < len(answer) else 0.0) for i, d in enumerate(direction)
        ]
        shifted = [0.0] + [-size * d for d in direction]
        residual = [
            s + (residual[i] if i < len(residual) else 0.0) for i, s in enumerate(shifted)
        ]
        if step + 1 < steps:
            following = inner(residual, residual, 0)
            ratio = following / current
            direction = [
                r + (ratio * direction[i] if i < len(direction) else 0.0)
                for i, r in enumerate(residual)
            ]
            current = following
    return answer, residual


def final_kernel(
    place_ref,
    moments_ref,
    first_ref,
    second_ref,
    third_ref,
    held_ref,
    even_in_ref,
    odd_in_ref,
    solution_ref,
    residual_ref,
    last_ref,
):
    sums = moments_ref[0]
    for source in range(1, moments_ref.shape[0]):
        sums = sums + moments_ref[source]
    sums = jnp.sum(sums, axis=1, keepdims=True)
    lanes = first_ref.shape[2]
    raw = [jnp.broadcast_to(sums[row : row + 1], (1, lanes)) for row in range(6)]
    unit = raw[0] / raw[1]
    scaled, factor = [], 1.0 / raw[0]
    for row in range(6):
        scaled.append(raw[row] * factor)
        factor = factor * unit
    answer, residual = coefficients(scaled, 3)
    power = jnp.ones_like(unit)
    answer_scaled, residual_scaled = [], []
    for row in range(4):
        residual_scaled.append(residual[row] * power)
        power = power * unit
        if row < 3:
            answer_scaled.append(answer[row] * power)
    is_even = lax.rem(place_ref[0], 2) == 0
    last_ref[...] = held_ref[pl.ds(HALO_BLOCKS, BLOCKS_DEV)]
    low, high = 0, BLOCKS_DEV - HALO_BLOCKS
    last_ref[pl.ds(jnp.where(is_even, high, low), HALO_BLOCKS)] += even_in_ref[...]
    last_ref[pl.ds(jnp.where(is_even, low, high), HALO_BLOCKS)] += odd_in_ref[...]
    for block in range(BLOCKS_DEV):
        first = first_ref[HALO_BLOCKS + block]
        second = second_ref[HALO_BLOCKS + block]
        third = third_ref[HALO_BLOCKS + block]
        last = last_ref[block]
        solution_ref[:, block, :] = (
            answer_scaled[0] * first + answer_scaled[1] * second + answer_scaled[2] * third
        )
        residual_ref[:, block, :] = (
            first
            + residual_scaled[1] * second
            + residual_scaled[2] * third
            + residual_scaled[3] * last
        )


def vmem(count):
    return [pl.BlockSpec(memory_space=pltpu.VMEM)] * count


def smem(count):
    return [pl.BlockSpec(memory_space=pltpu.SMEM)] * count


def shards(fibre_data, kernels, block_index, live_count):
    tiles, devices = lax.axis_size("tile"), lax.axis_size("tile") * lax.axis_size("wave")
    _, groups, slots, spaxels, fibres = kernels.shape
    waves = fibre_data.shape[0]
    tile = lax.axis_index("tile")
    first_block = tile * BLOCKS_DEV - HALO_BLOCKS
    index = (block_index - first_block).reshape(groups * slots)
    place = jnp.stack([tile, live_count[0]])
    weights = kernels.reshape(groups, slots, spaxels, fibres)
    data = jnp.swapaxes(fibre_data, 0, 1)
    window = jax.ShapeDtypeStruct((EXTENT, waves, spaxels), jnp.float32)
    rim = jax.ShapeDtypeStruct((RIM, waves, spaxels), jnp.float32)
    half_rim = jax.ShapeDtypeStruct((HALO_BLOCKS, waves, spaxels), jnp.float32)
    moment = jax.ShapeDtypeStruct((MOMENT_ROWS, spaxels), jnp.float32)
    moment_all = jax.ShapeDtypeStruct((devices, MOMENT_ROWS, spaxels), jnp.float32)
    params = pltpu.CompilerParams(vmem_limit_bytes=VMEM_LIMIT)
    even_pairs = [(i, i ^ 1) for i in range(tiles) if (i ^ 1) < tiles]
    odd_pairs = [
        (i, j) for i in range(tiles) for j in [((i + 1) ^ 1) - 1] if 0 <= j < tiles
    ]

    def swap(even, odd):
        return lax.ppermute(even, "tile", even_pairs), lax.ppermute(odd, "tile", odd_pairs)

    held, even, odd = pl.pallas_call(
        rhs_kernel,
        out_shape=(window, rim, rim),
        in_specs=smem(2) + vmem(2),
        out_specs=tuple(vmem(3)),
        compiler_params=params,
        name="rhs",
    )(place, index, data, weights)
    moments = jnp.zeros(moment.shape, jnp.float32)
    vectors = []
    for power in range(3):
        final = power == 2
        even, odd = swap(even, odd)
        out_rim = half_rim if final else rim
        vector, held, even, odd, moments = pl.pallas_call(
            functools.partial(step_kernel, power, final),
            out_shape=(window, window, out_rim, out_rim, moment_all if final else moment),
            in_specs=smem(2) + vmem(5),
            out_specs=tuple(vmem(5)),
            scratch_shapes=[pltpu.VMEM((EXTENT, 2 * waves, spaxels), jnp.bfloat16)],
            compiler_params=params,
            name=f"step{power}",
        )(place, index, held, even, odd, moments, weights)
        vectors.append(vector)
    even, odd = swap(even, odd)
    moments = lax.all_to_all(moments, ("tile", "wave"), 0, 0)
    out = jax.ShapeDtypeStruct((waves, BLOCKS_DEV, spaxels), jnp.float32)
    return pl.pallas_call(
        final_kernel,
        out_shape=(out, out),
        in_specs=smem(1) + vmem(7),
        out_specs=tuple(vmem(2)),
        scratch_shapes=[pltpu.VMEM((BLOCKS_DEV, waves, spaxels), jnp.float32)],
        compiler_params=params,
        name="combine",
    )(place, moments, *vectors, held, even, odd)


def solution(mesh):
    in_specs = (
        P("wave", "tile", None),
        P("wave", "tile", None, None, None),
        P("wave", "tile", None),
        P("tile"),
    )
    out_specs = (P("wave", "tile", None), P("wave", "tile", None))
    return jax.shard_map(shards, mesh=mesh, in_specs=in_specs, out_specs=out_specs, check_vma=False)
```

```python
import functools

import jax
import jax.numpy as jnp
from jax import lax
from jax.experimental import pallas as pl
from jax.experimental.pallas import tpu as pltpu
from jax.sharding import PartitionSpec as P

HALO_BLOCKS = 4
BLOCKS_DEV = 16
EXTENT = BLOCKS_DEV + 2 * HALO_BLOCKS
RIM = 2 * HALO_BLOCKS
TIKHONOV = 0.5
CHUNKS = 8
MOMENT_ROWS = 8
VMEM_LIMIT = 24 * 1024 * 1024


def split(value):
    upper = value.astype(jnp.bfloat16)
    lower = (value - upper.astype(jnp.float32)).astype(jnp.bfloat16)
    return upper, lower


def halves_sum(value):
    half = value.shape[0] // 2
    return value[:half] + value[half:]


def scatter(spread, place_ref, index_ref, group, partial_ref):
    lanes = partial_ref.shape[2]
    first = place_ref[0] * BLOCKS_DEV - HALO_BLOCKS
    for slot in range(index_ref.shape[1]):
        block = index_ref[group, slot] - first
        partial_ref[block] += spread[:, slot * lanes : (slot + 1) * lanes]


def spread_of(image, weights):
    return lax.dot_general(
        image, weights, (((1,), (1,)), ((), ())), preferred_element_type=jnp.float32
    )


def emit_rims(place_ref, partial_ref, even_ref, odd_ref):
    width = even_ref.shape[0]
    top = EXTENT - width
    is_even = lax.rem(place_ref[0], 2) == 0
    even_ref[...] = partial_ref[pl.ds(jnp.where(is_even, top, 0), width)]
    odd_ref[...] = partial_ref[pl.ds(jnp.where(is_even, 0, top), width)]


def rhs_kernel(
    place_ref,
    live_ref,
    index_ref,
    data_ref,
    source_ref,
    kernels_ref,
    partial_ref,
    even_ref,
    odd_ref,
    narrow_ref,
    wide_ref,
    sems,
    data_sem,
):
    groups, slots, spaxels, fibres = kernels_ref.shape
    chunks = sems.shape[0]
    size = groups // chunks

    def copy(chunk):
        part = pl.ds(chunk * size, size)
        return pltpu.make_async_copy(source_ref.at[part], kernels_ref.at[part], sems.at[chunk])

    data_copy = pltpu.make_async_copy(data_ref, narrow_ref, data_sem)
    data_copy.start()
    for chunk in range(chunks):
        copy(chunk).start()
    partial_ref[...] = jnp.zeros_like(partial_ref)
    data_copy.wait()
    wide_ref[...] = narrow_ref[...].astype(jnp.float32)
    live = live_ref[0]
    for chunk in range(chunks):
        copy(chunk).wait()
        for group in range(chunk * size, (chunk + 1) * size):
            data = jnp.where(group < live, wide_ref[:, group, :], 0.0).astype(jnp.bfloat16)
            spread = spread_of(data, kernels_ref[group].reshape(slots * spaxels, fibres))
            scatter(spread, place_ref, index_ref, group, partial_ref)
    emit_rims(place_ref, partial_ref, even_ref, odd_ref)


def step_kernel(
    power,
    final,
    place_ref,
    live_ref,
    index_ref,
    held_ref,
    even_in_ref,
    odd_in_ref,
    moments_in_ref,
    kernels_ref,
    vector_ref,
    partial_ref,
    even_ref,
    odd_ref,
    moments_ref,
    operand_ref,
    image_ref,
):
    groups, slots, spaxels, fibres = kernels_ref.shape
    waves = held_ref.shape[1]
    live = live_ref[0]
    is_even = lax.rem(place_ref[0], 2) == 0
    first_block = place_ref[0] * BLOCKS_DEV - HALO_BLOCKS
    top = EXTENT - RIM
    vector_ref[...] = held_ref[...]
    vector_ref[pl.ds(jnp.where(is_even, top, 0), RIM)] += even_in_ref[...]
    vector_ref[pl.ds(jnp.where(is_even, 0, top), RIM)] += odd_in_ref[...]
    square = jnp.zeros(vector_ref.shape[1:], jnp.float32)
    for block in range(EXTENT):
        value = vector_ref[block]
        operand_ref[block, :waves], operand_ref[block, waves:] = split(value)
        if HALO_BLOCKS <= block < HALO_BLOCKS + BLOCKS_DEV:
            square = square + value * value
    partial_ref[...] = jnp.zeros_like(partial_ref)
    energy = jnp.zeros((waves, fibres), jnp.float32)
    for group in range(groups):
        picked = jnp.concatenate(
            [operand_ref[index_ref[group, slot] - first_block] for slot in range(slots)], axis=1
        )
        weights = kernels_ref[group].reshape(slots * spaxels, fibres)
        image = halves_sum(jnp.dot(picked, weights, preferred_element_type=jnp.float32))
        image = jnp.where(group < live, image, 0.0)
        energy = energy + image * image
        image_ref[group, :waves], image_ref[group, waves:] = split(image)
    for group in range(groups):
        weights = kernels_ref[group].reshape(slots * spaxels, fibres)
        spread = halves_sum(spread_of(image_ref[group], weights))
        scatter(spread, place_ref, index_ref, group, partial_ref)
    emit_rims(place_ref, partial_ref, even_ref, odd_ref)
    for block in range(EXTENT):
        partial_ref[block] += TIKHONOV * vector_ref[block]
    square_row = jnp.sum(square, axis=0, keepdims=True)
    energy_row = jnp.sum(energy, axis=0, keepdims=True) + TIKHONOV * square_row
    rows = lax.broadcasted_iota(jnp.int32, moments_in_ref.shape, 0)
    moments = jnp.where(
        rows == 2 * power,
        square_row,
        jnp.where(rows == 2 * power + 1, energy_row, moments_in_ref[...]),
    )
    moments_ref[...] = jnp.broadcast_to(moments, moments_ref.shape) if final else moments


def coefficients(moments, steps):
    def inner(first, second, shift):
        total = 0.0
        for i, a in enumerate(first):
            for j, b in enumerate(second):
                if a is not None and b is not None:
                    total = total + a * b * moments[i + j + shift]
        return total

    one = jnp.ones_like(moments[0])
    residual, direction = [one], [one]
    answer = []
    current = inner(residual, residual, 0)
    for step in range(steps):
        size = current / inner(direction, direction, 1)
        answer = [
            size * d + (answer[i] if i < len(answer) else 0.0) for i, d in enumerate(direction)
        ]
        shifted = [0.0] + [-size * d for d in direction]
        residual = [
            s + (residual[i] if i < len(residual) else 0.0) for i, s in enumerate(shifted)
        ]
        if step + 1 < steps:
            following = inner(residual, residual, 0)
            ratio = following / current
            direction = [
                r + (ratio * direction[i] if i < len(direction) else 0.0)
                for i, r in enumerate(residual)
            ]
            current = following
    return answer, residual


def final_kernel(
    place_ref,
    moments_ref,
    first_ref,
    second_ref,
    third_ref,
    held_ref,
    even_in_ref,
    odd_in_ref,
    solution_ref,
    residual_ref,
    last_ref,
):
    sums = moments_ref[0]
    for source in range(1, moments_ref.shape[0]):
        sums = sums + moments_ref[source]
    sums = jnp.sum(sums, axis=1, keepdims=True)
    lanes = first_ref.shape[2]
    raw = [jnp.broadcast_to(sums[row : row + 1], (1, lanes)) for row in range(6)]
    unit = raw[0] / raw[1]
    scaled, factor = [], 1.0 / raw[0]
    for row in range(6):
        scaled.append(raw[row] * factor)
        factor = factor * unit
    answer, residual = coefficients(scaled, 3)
    power = jnp.ones_like(unit)
    answer_scaled, residual_scaled = [], []
    for row in range(4):
        residual_scaled.append(residual[row] * power)
        power = power * unit
        if row < 3:
            answer_scaled.append(answer[row] * power)
    is_even = lax.rem(place_ref[0], 2) == 0
    last_ref[...] = held_ref[pl.ds(HALO_BLOCKS, BLOCKS_DEV)]
    low, high = 0, BLOCKS_DEV - HALO_BLOCKS
    last_ref[pl.ds(jnp.where(is_even, high, low), HALO_BLOCKS)] += even_in_ref[...]
    last_ref[pl.ds(jnp.where(is_even, low, high), HALO_BLOCKS)] += odd_in_ref[...]
    for block in range(BLOCKS_DEV):
        first = first_ref[HALO_BLOCKS + block]
        second = second_ref[HALO_BLOCKS + block]
        third = third_ref[HALO_BLOCKS + block]
        last = last_ref[block]
        solution_ref[:, block, :] = (
            answer_scaled[0] * first + answer_scaled[1] * second + answer_scaled[2] * third
        )
        residual_ref[:, block, :] = (
            first
            + residual_scaled[1] * second
            + residual_scaled[2] * third
            + residual_scaled[3] * last
        )


def vmem(count):
    return [pl.BlockSpec(memory_space=pltpu.VMEM)] * count


def smem(count):
    return [pl.BlockSpec(memory_space=pltpu.SMEM)] * count


def shards(fibre_data, kernels, block_index, live_count):
    tiles, devices = lax.axis_size("tile"), lax.axis_size("tile") * lax.axis_size("wave")
    _, groups, slots, spaxels, fibres = kernels.shape
    waves = fibre_data.shape[0]
    place = lax.axis_index("tile").reshape(1)
    index = block_index.reshape(groups, slots)
    weights = kernels.reshape(groups, slots, spaxels, fibres)
    window = jax.ShapeDtypeStruct((EXTENT, waves, spaxels), jnp.float32)
    rim = jax.ShapeDtypeStruct((RIM, waves, spaxels), jnp.float32)
    half_rim = jax.ShapeDtypeStruct((HALO_BLOCKS, waves, spaxels), jnp.float32)
    moment = jax.ShapeDtypeStruct((MOMENT_ROWS, spaxels), jnp.float32)
    moment_all = jax.ShapeDtypeStruct((devices, MOMENT_ROWS, spaxels), jnp.float32)
    params = pltpu.CompilerParams(vmem_limit_bytes=VMEM_LIMIT)
    even_pairs = [(i, i ^ 1) for i in range(tiles) if (i ^ 1) < tiles]
    odd_pairs = [
        (i, j) for i in range(tiles) for j in [((i + 1) ^ 1) - 1] if 0 <= j < tiles
    ]

    def swap(even, odd):
        return lax.ppermute(even, "tile", even_pairs), lax.ppermute(odd, "tile", odd_pairs)

    chunks = CHUNKS if groups % CHUNKS == 0 else 1
    weights, held, even, odd = pl.pallas_call(
        rhs_kernel,
        out_shape=(jax.ShapeDtypeStruct(weights.shape, weights.dtype), window, rim, rim),
        in_specs=smem(3) + [pl.BlockSpec(memory_space=pltpu.HBM)] * 2,
        out_specs=tuple(vmem(4)),
        scratch_shapes=[
            pltpu.VMEM(fibre_data.shape, fibre_data.dtype),
            pltpu.VMEM(fibre_data.shape, jnp.float32),
            pltpu.SemaphoreType.DMA((chunks,)),
            pltpu.SemaphoreType.DMA,
        ],
        compiler_params=params,
        name="rhs",
    )(place, live_count, index, fibre_data, weights)
    moments = jnp.zeros(moment.shape, jnp.float32)
    vectors = []
    for power in range(3):
        final = power == 2
        even, odd = swap(even, odd)
        out_rim = half_rim if final else rim
        vector, held, even, odd, moments = pl.pallas_call(
            functools.partial(step_kernel, power, final),
            out_shape=(window, window, out_rim, out_rim, moment_all if final else moment),
            in_specs=smem(3) + vmem(5),
            out_specs=tuple(vmem(5)),
            scratch_shapes=[
                pltpu.VMEM((EXTENT, 2 * waves, spaxels), jnp.bfloat16),
                pltpu.VMEM((groups, 2 * waves, fibres), jnp.bfloat16),
            ],
            compiler_params=params,
            name=f"step{power}",
        )(place, live_count, index, held, even, odd, moments, weights)
        vectors.append(vector)
    even, odd = swap(even, odd)
    moments = lax.all_to_all(moments, ("tile", "wave"), 0, 0)
    out = jax.ShapeDtypeStruct((waves, BLOCKS_DEV, spaxels), jnp.float32)
    return pl.pallas_call(
        final_kernel,
        out_shape=(out, out),
        in_specs=smem(1) + vmem(7),
        out_specs=tuple(vmem(2)),
        scratch_shapes=[pltpu.VMEM((BLOCKS_DEV, waves, spaxels), jnp.float32)],
        compiler_params=params,
        name="combine",
    )(place, moments, *vectors, held, even, odd)


def solution(mesh):
    in_specs = (
        P("wave", "tile", None),
        P("wave", "tile", None, None, None),
        P("wave", "tile", None),
        P("tile"),
    )
    out_specs = (P("wave", "tile", None), P("wave", "tile", None))
    return jax.shard_map(shards, mesh=mesh, in_specs=in_specs, out_specs=out_specs, check_vma=False)
```

```python
import functools

import jax
import jax.numpy as jnp
from jax import lax
from jax.experimental import pallas as pl
from jax.experimental.pallas import tpu as pltpu
from jax.sharding import PartitionSpec as P

HALO_BLOCKS = 4
BLOCKS_DEV = 16
EXTENT = BLOCKS_DEV + 2 * HALO_BLOCKS
RIM = 2 * HALO_BLOCKS
TIKHONOV = 0.5
CHUNKS = 8
MOMENT_ROWS = 8
VMEM_LIMIT = 24 * 1024 * 1024


def split(value):
    upper = value.astype(jnp.bfloat16)
    lower = (value - upper.astype(jnp.float32)).astype(jnp.bfloat16)
    return upper, lower


def halves_sum(value):
    half = value.shape[0] // 2
    return value[:half] + value[half:]


def scatter(spread, place_ref, index_ref, group, partial_ref):
    lanes = partial_ref.shape[2]
    first = place_ref[0] * BLOCKS_DEV - HALO_BLOCKS
    for slot in range(index_ref.shape[0]):
        block = index_ref[slot, group] - first
        partial_ref[block] += spread[:, slot * lanes : (slot + 1) * lanes]


def spread_of(image, weights):
    return lax.dot_general(
        image, weights, (((1,), (1,)), ((), ())), preferred_element_type=jnp.float32
    )


def emit_rims(place_ref, partial_ref, even_ref, odd_ref):
    width = even_ref.shape[0]
    top = EXTENT - width
    is_even = lax.rem(place_ref[0], 2) == 0
    even_ref[...] = partial_ref[pl.ds(jnp.where(is_even, top, 0), width)]
    odd_ref[...] = partial_ref[pl.ds(jnp.where(is_even, 0, top), width)]


def rhs_kernel(
    place_ref,
    live_ref,
    index_ref,
    data_ref,
    source_ref,
    kernels_ref,
    partial_ref,
    even_ref,
    odd_ref,
    narrow_ref,
    wide_ref,
    sems,
    data_sem,
):
    groups, slots, spaxels, fibres = kernels_ref.shape
    chunks = sems.shape[0]
    size = groups // chunks

    def copy(chunk):
        part = pl.ds(chunk * size, size)
        return pltpu.make_async_copy(source_ref.at[part], kernels_ref.at[part], sems.at[chunk])

    data_copy = pltpu.make_async_copy(data_ref, narrow_ref, data_sem)
    data_copy.start()
    for chunk in range(chunks):
        copy(chunk).start()
    partial_ref[...] = jnp.zeros_like(partial_ref)
    data_copy.wait()
    wide_ref[...] = narrow_ref[...].astype(jnp.float32)
    live = live_ref[0]
    for chunk in range(chunks):
        copy(chunk).wait()
        for group in range(chunk * size, (chunk + 1) * size):
            data = jnp.where(group < live, wide_ref[:, group, :], 0.0).astype(jnp.bfloat16)
            spread = spread_of(data, kernels_ref[group].reshape(slots * spaxels, fibres))
            scatter(spread, place_ref, index_ref, group, partial_ref)
    emit_rims(place_ref, partial_ref, even_ref, odd_ref)


def step_kernel(
    power,
    final,
    place_ref,
    live_ref,
    index_ref,
    held_ref,
    even_in_ref,
    odd_in_ref,
    moments_in_ref,
    kernels_ref,
    vector_ref,
    partial_ref,
    even_ref,
    odd_ref,
    moments_ref,
    operand_ref,
    image_ref,
):
    groups, slots, spaxels, fibres = kernels_ref.shape
    waves = held_ref.shape[1]
    live = live_ref[0]
    is_even = lax.rem(place_ref[0], 2) == 0
    first_block = place_ref[0] * BLOCKS_DEV - HALO_BLOCKS
    top = EXTENT - RIM
    vector_ref[...] = held_ref[...]
    vector_ref[pl.ds(jnp.where(is_even, top, 0), RIM)] += even_in_ref[...]
    vector_ref[pl.ds(jnp.where(is_even, 0, top), RIM)] += odd_in_ref[...]
    square = jnp.zeros(vector_ref.shape[1:], jnp.float32)
    for block in range(EXTENT):
        value = vector_ref[block]
        operand_ref[block, :waves], operand_ref[block, waves:] = split(value)
        if HALO_BLOCKS <= block < HALO_BLOCKS + BLOCKS_DEV:
            square = square + value * value
    partial_ref[...] = jnp.zeros_like(partial_ref)
    energy = jnp.zeros((waves, fibres), jnp.float32)
    for group in range(groups):
        picked = jnp.concatenate(
            [operand_ref[index_ref[slot, group] - first_block] for slot in range(slots)], axis=1
        )
        weights = kernels_ref[group].reshape(slots * spaxels, fibres)
        image = halves_sum(jnp.dot(picked, weights, preferred_element_type=jnp.float32))
        image = jnp.where(group < live, image, 0.0)
        energy = energy + image * image
        image_ref[group, :waves], image_ref[group, waves:] = split(image)
    for group in range(groups):
        weights = kernels_ref[group].reshape(slots * spaxels, fibres)
        spread = halves_sum(spread_of(image_ref[group], weights))
        scatter(spread, place_ref, index_ref, group, partial_ref)
    emit_rims(place_ref, partial_ref, even_ref, odd_ref)
    for block in range(EXTENT):
        partial_ref[block] += TIKHONOV * vector_ref[block]
    square_row = jnp.sum(square, axis=0, keepdims=True)
    energy_row = jnp.sum(energy, axis=0, keepdims=True) + TIKHONOV * square_row
    rows = lax.broadcasted_iota(jnp.int32, moments_in_ref.shape, 0)
    moments = jnp.where(
        rows == 2 * power,
        square_row,
        jnp.where(rows == 2 * power + 1, energy_row, moments_in_ref[...]),
    )
    moments_ref[...] = jnp.broadcast_to(moments, moments_ref.shape) if final else moments


def coefficients(moments, steps):
    def inner(first, second, shift):
        total = 0.0
        for i, a in enumerate(first):
            for j, b in enumerate(second):
                if a is not None and b is not None:
                    total = total + a * b * moments[i + j + shift]
        return total

    one = jnp.ones_like(moments[0])
    residual, direction = [one], [one]
    answer = []
    current = inner(residual, residual, 0)
    for step in range(steps):
        size = current / inner(direction, direction, 1)
        answer = [
            size * d + (answer[i] if i < len(answer) else 0.0) for i, d in enumerate(direction)
        ]
        shifted = [0.0] + [-size * d for d in direction]
        residual = [
            s + (residual[i] if i < len(residual) else 0.0) for i, s in enumerate(shifted)
        ]
        if step + 1 < steps:
            following = inner(residual, residual, 0)
            ratio = following / current
            direction = [
                r + (ratio * direction[i] if i < len(direction) else 0.0)
                for i, r in enumerate(residual)
            ]
            current = following
    return answer, residual


def final_kernel(
    place_ref,
    moments_ref,
    first_ref,
    second_ref,
    third_ref,
    held_ref,
    even_in_ref,
    odd_in_ref,
    solution_ref,
    residual_ref,
    last_ref,
):
    sums = moments_ref[0]
    for source in range(1, moments_ref.shape[0]):
        sums = sums + moments_ref[source]
    sums = jnp.sum(sums, axis=1, keepdims=True)
    lanes = first_ref.shape[2]
    raw = [jnp.broadcast_to(sums[row : row + 1], (1, lanes)) for row in range(6)]
    unit = raw[0] / raw[1]
    scaled, factor = [], 1.0 / raw[0]
    for row in range(6):
        scaled.append(raw[row] * factor)
        factor = factor * unit
    answer, residual = coefficients(scaled, 3)
    power = jnp.ones_like(unit)
    answer_scaled, residual_scaled = [], []
    for row in range(4):
        residual_scaled.append(residual[row] * power)
        power = power * unit
        if row < 3:
            answer_scaled.append(answer[row] * power)
    is_even = lax.rem(place_ref[0], 2) == 0
    last_ref[...] = held_ref[pl.ds(HALO_BLOCKS, BLOCKS_DEV)]
    low, high = 0, BLOCKS_DEV - HALO_BLOCKS
    last_ref[pl.ds(jnp.where(is_even, high, low), HALO_BLOCKS)] += even_in_ref[...]
    last_ref[pl.ds(jnp.where(is_even, low, high), HALO_BLOCKS)] += odd_in_ref[...]
    for block in range(BLOCKS_DEV):
        first = first_ref[HALO_BLOCKS + block]
        second = second_ref[HALO_BLOCKS + block]
        third = third_ref[HALO_BLOCKS + block]
        last = last_ref[block]
        solution_ref[:, block, :] = (
            answer_scaled[0] * first + answer_scaled[1] * second + answer_scaled[2] * third
        )
        residual_ref[:, block, :] = (
            first
            + residual_scaled[1] * second
            + residual_scaled[2] * third
            + residual_scaled[3] * last
        )


def vmem(count):
    return [pl.BlockSpec(memory_space=pltpu.VMEM)] * count


def smem(count):
    return [pl.BlockSpec(memory_space=pltpu.SMEM)] * count


def shards(fibre_data, kernels, block_index, live_count):
    tiles, devices = lax.axis_size("tile"), lax.axis_size("tile") * lax.axis_size("wave")
    _, groups, slots, spaxels, fibres = kernels.shape
    waves = fibre_data.shape[0]
    place = lax.axis_index("tile").reshape(1)
    index = jnp.swapaxes(block_index, 1, 2).reshape(slots, groups)
    weights = kernels.reshape(groups, slots, spaxels, fibres)
    window = jax.ShapeDtypeStruct((EXTENT, waves, spaxels), jnp.float32)
    rim = jax.ShapeDtypeStruct((RIM, waves, spaxels), jnp.float32)
    half_rim = jax.ShapeDtypeStruct((HALO_BLOCKS, waves, spaxels), jnp.float32)
    moment = jax.ShapeDtypeStruct((MOMENT_ROWS, spaxels), jnp.float32)
    moment_all = jax.ShapeDtypeStruct((devices, MOMENT_ROWS, spaxels), jnp.float32)
    params = pltpu.CompilerParams(vmem_limit_bytes=VMEM_LIMIT)
    even_pairs = [(i, i ^ 1) for i in range(tiles) if (i ^ 1) < tiles]
    odd_pairs = [
        (i, j) for i in range(tiles) for j in [((i + 1) ^ 1) - 1] if 0 <= j < tiles
    ]

    def swap(even, odd):
        return lax.ppermute(even, "tile", even_pairs), lax.ppermute(odd, "tile", odd_pairs)

    chunks = CHUNKS if groups % CHUNKS == 0 else 1
    weights, held, even, odd = pl.pallas_call(
        rhs_kernel,
        out_shape=(jax.ShapeDtypeStruct(weights.shape, weights.dtype), window, rim, rim),
        in_specs=smem(3) + [pl.BlockSpec(memory_space=pltpu.HBM)] * 2,
        out_specs=tuple(vmem(4)),
        scratch_shapes=[
            pltpu.VMEM(fibre_data.shape, fibre_data.dtype),
            pltpu.VMEM(fibre_data.shape, jnp.float32),
            pltpu.SemaphoreType.DMA((chunks,)),
            pltpu.SemaphoreType.DMA,
        ],
        compiler_params=params,
        name="rhs",
    )(
        place,
        live_count,
        index,
        pltpu.with_memory_space_constraint(fibre_data, pltpu.HBM),
        pltpu.with_memory_space_constraint(weights, pltpu.HBM),
    )
    moments = jnp.zeros(moment.shape, jnp.float32)
    vectors = []
    for power in range(3):
        final = power == 2
        even, odd = swap(even, odd)
        out_rim = half_rim if final else rim
        vector, held, even, odd, moments = pl.pallas_call(
            functools.partial(step_kernel, power, final),
            out_shape=(window, window, out_rim, out_rim, moment_all if final else moment),
            in_specs=smem(3) + vmem(5),
            out_specs=tuple(vmem(5)),
            scratch_shapes=[
                pltpu.VMEM((EXTENT, 2 * waves, spaxels), jnp.bfloat16),
                pltpu.VMEM((groups, 2 * waves, fibres), jnp.bfloat16),
            ],
            compiler_params=params,
            name=f"step{power}",
        )(place, live_count, index, held, even, odd, moments, weights)
        vectors.append(vector)
    even, odd = swap(even, odd)
    moments = lax.all_to_all(moments, ("tile", "wave"), 0, 0)
    out = jax.ShapeDtypeStruct((waves, BLOCKS_DEV, spaxels), jnp.float32)
    return pl.pallas_call(
        final_kernel,
        out_shape=(out, out),
        in_specs=smem(1) + vmem(7),
        out_specs=tuple(vmem(2)),
        scratch_shapes=[pltpu.VMEM((BLOCKS_DEV, waves, spaxels), jnp.float32)],
        compiler_params=params,
        name="combine",
    )(place, moments, *vectors, held, even, odd)


def solution(mesh):
    in_specs = (
        P("wave", "tile", None),
        P("wave", "tile", None, None, None),
        P("wave", "tile", None),
        P("tile"),
    )
    out_specs = (P("wave", "tile", None), P("wave", "tile", None))
    return jax.shard_map(shards, mesh=mesh, in_specs=in_specs, out_specs=out_specs, check_vma=False)
```

```python
import functools

import jax
import jax.numpy as jnp
from jax import lax
from jax.experimental import pallas as pl
from jax.experimental.pallas import tpu as pltpu
from jax.sharding import PartitionSpec as P

HALO_BLOCKS = 4
BLOCKS_DEV = 16
EXTENT = BLOCKS_DEV + 2 * HALO_BLOCKS
RIM = 2 * HALO_BLOCKS
TIKHONOV = 0.5
CHUNKS = 2
MOMENT_ROWS = 8
VMEM_LIMIT = 24 * 1024 * 1024


def split(value):
    upper = value.astype(jnp.bfloat16)
    lower = (value - upper.astype(jnp.float32)).astype(jnp.bfloat16)
    return upper, lower


def halves_sum(value):
    half = value.shape[0] // 2
    return value[:half] + value[half:]


def scatter(spread, place_ref, index_ref, group, partial_ref):
    lanes = partial_ref.shape[2]
    first = place_ref[0] * BLOCKS_DEV - HALO_BLOCKS
    for slot in range(index_ref.shape[0]):
        block = index_ref[slot, group] - first
        partial_ref[block] += spread[:, slot * lanes : (slot + 1) * lanes]


def spread_of(image, weights):
    return lax.dot_general(
        image, weights, (((1,), (1,)), ((), ())), preferred_element_type=jnp.float32
    )


def emit_rims(partial_ref, upper_ref, lower_ref):
    width = upper_ref.shape[0]
    upper_ref[...] = partial_ref[EXTENT - width :]
    lower_ref[...] = partial_ref[:width]


def add_rims(tiles, place_ref, target_ref, from_below_ref, from_above_ref):
    width = from_below_ref.shape[0]
    tile = place_ref[0]

    @pl.when(tile > 0)
    def _():
        target_ref[:width] += from_below_ref[...]

    @pl.when(tile < tiles - 1)
    def _():
        target_ref[target_ref.shape[0] - width :] += from_above_ref[...]


def rhs_kernel(
    place_ref,
    live_ref,
    index_ref,
    data_ref,
    source_ref,
    kernels_ref,
    partial_ref,
    upper_ref,
    lower_ref,
    narrow_ref,
    wide_ref,
    sems,
    data_sem,
):
    groups, slots, spaxels, fibres = kernels_ref.shape
    chunks = sems.shape[0]
    size = groups // chunks

    def copy(chunk):
        part = pl.ds(chunk * size, size)
        return pltpu.make_async_copy(source_ref.at[part], kernels_ref.at[part], sems.at[chunk])

    data_copy = pltpu.make_async_copy(data_ref, narrow_ref, data_sem)
    data_copy.start()
    for chunk in range(chunks):
        copy(chunk).start()
    partial_ref[...] = jnp.zeros_like(partial_ref)
    data_copy.wait()
    wide_ref[...] = narrow_ref[...].astype(jnp.float32)
    live = live_ref[0]
    for chunk in range(chunks):
        copy(chunk).wait()
        for group in range(chunk * size, (chunk + 1) * size):
            data = jnp.where(group < live, wide_ref[:, group, :], 0.0).astype(jnp.bfloat16)
            spread = spread_of(data, kernels_ref[group].reshape(slots * spaxels, fibres))
            scatter(spread, place_ref, index_ref, group, partial_ref)
    emit_rims(partial_ref, upper_ref, lower_ref)


def step_kernel(
    tiles,
    power,
    final,
    place_ref,
    live_ref,
    index_ref,
    held_ref,
    from_below_ref,
    from_above_ref,
    moments_in_ref,
    kernels_ref,
    vector_ref,
    partial_ref,
    upper_ref,
    lower_ref,
    moments_ref,
    operand_ref,
    image_ref,
):
    groups, slots, spaxels, fibres = kernels_ref.shape
    waves = held_ref.shape[1]
    live = live_ref[0]
    first_block = place_ref[0] * BLOCKS_DEV - HALO_BLOCKS
    vector_ref[...] = held_ref[...]
    add_rims(tiles, place_ref, vector_ref, from_below_ref, from_above_ref)
    square = jnp.zeros(vector_ref.shape[1:], jnp.float32)
    for block in range(EXTENT):
        value = vector_ref[block]
        operand_ref[block, :waves], operand_ref[block, waves:] = split(value)
        if HALO_BLOCKS <= block < HALO_BLOCKS + BLOCKS_DEV:
            square = square + value * value
    partial_ref[...] = jnp.zeros_like(partial_ref)
    energy = jnp.zeros((waves, fibres), jnp.float32)
    for group in range(groups):
        picked = jnp.concatenate(
            [operand_ref[index_ref[slot, group] - first_block] for slot in range(slots)], axis=1
        )
        weights = kernels_ref[group].reshape(slots * spaxels, fibres)
        image = halves_sum(jnp.dot(picked, weights, preferred_element_type=jnp.float32))
        image = jnp.where(group < live, image, 0.0)
        energy = energy + image * image
        image_ref[group, :waves], image_ref[group, waves:] = split(image)
    for group in range(groups):
        weights = kernels_ref[group].reshape(slots * spaxels, fibres)
        spread = halves_sum(spread_of(image_ref[group], weights))
        scatter(spread, place_ref, index_ref, group, partial_ref)
    emit_rims(partial_ref, upper_ref, lower_ref)
    for block in range(EXTENT):
        partial_ref[block] += TIKHONOV * vector_ref[block]
    square_row = jnp.sum(square, axis=0, keepdims=True)
    energy_row = jnp.sum(energy, axis=0, keepdims=True) + TIKHONOV * square_row
    rows = lax.broadcasted_iota(jnp.int32, moments_in_ref.shape, 0)
    moments = jnp.where(
        rows == 2 * power,
        square_row,
        jnp.where(rows == 2 * power + 1, energy_row, moments_in_ref[...]),
    )
    moments_ref[...] = jnp.broadcast_to(moments, moments_ref.shape) if final else moments


def coefficients(moments, steps):
    def inner(first, second, shift):
        total = 0.0
        for i, a in enumerate(first):
            for j, b in enumerate(second):
                if a is not None and b is not None:
                    total = total + a * b * moments[i + j + shift]
        return total

    one = jnp.ones_like(moments[0])
    residual, direction = [one], [one]
    answer = []
    current = inner(residual, residual, 0)
    for step in range(steps):
        size = current / inner(direction, direction, 1)
        answer = [
            size * d + (answer[i] if i < len(answer) else 0.0) for i, d in enumerate(direction)
        ]
        shifted = [0.0] + [-size * d for d in direction]
        residual = [
            s + (residual[i] if i < len(residual) else 0.0) for i, s in enumerate(shifted)
        ]
        if step + 1 < steps:
            following = inner(residual, residual, 0)
            ratio = following / current
            direction = [
                r + (ratio * direction[i] if i < len(direction) else 0.0)
                for i, r in enumerate(residual)
            ]
            current = following
    return answer, residual


def final_kernel(
    tiles,
    place_ref,
    moments_ref,
    first_ref,
    second_ref,
    third_ref,
    held_ref,
    from_below_ref,
    from_above_ref,
    solution_ref,
    residual_ref,
    last_ref,
):
    sums = moments_ref[0]
    for source in range(1, moments_ref.shape[0]):
        sums = sums + moments_ref[source]
    sums = jnp.sum(sums, axis=1, keepdims=True)
    lanes = first_ref.shape[2]
    raw = [jnp.broadcast_to(sums[row : row + 1], (1, lanes)) for row in range(6)]
    unit = raw[0] / raw[1]
    scaled, factor = [], 1.0 / raw[0]
    for row in range(6):
        scaled.append(raw[row] * factor)
        factor = factor * unit
    answer, residual = coefficients(scaled, 3)
    power = jnp.ones_like(unit)
    answer_scaled, residual_scaled = [], []
    for row in range(4):
        residual_scaled.append(residual[row] * power)
        power = power * unit
        if row < 3:
            answer_scaled.append(answer[row] * power)
    last_ref[...] = held_ref[pl.ds(HALO_BLOCKS, BLOCKS_DEV)]
    add_rims(tiles, place_ref, last_ref, from_below_ref, from_above_ref)
    for block in range(BLOCKS_DEV):
        first = first_ref[HALO_BLOCKS + block]
        second = second_ref[HALO_BLOCKS + block]
        third = third_ref[HALO_BLOCKS + block]
        last = last_ref[block]
        solution_ref[:, block, :] = (
            answer_scaled[0] * first + answer_scaled[1] * second + answer_scaled[2] * third
        )
        residual_ref[:, block, :] = (
            first
            + residual_scaled[1] * second
            + residual_scaled[2] * third
            + residual_scaled[3] * last
        )


def vmem(count):
    return [pl.BlockSpec(memory_space=pltpu.VMEM)] * count


def smem(count):
    return [pl.BlockSpec(memory_space=pltpu.SMEM)] * count


def shards(fibre_data, kernels, block_index, live_count):
    tiles, devices = lax.axis_size("tile"), lax.axis_size("tile") * lax.axis_size("wave")
    _, groups, slots, spaxels, fibres = kernels.shape
    waves = fibre_data.shape[0]
    place = lax.axis_index("tile").reshape(1)
    index = jnp.swapaxes(block_index, 1, 2).reshape(slots, groups)
    weights = kernels.reshape(groups, slots, spaxels, fibres)
    window = jax.ShapeDtypeStruct((EXTENT, waves, spaxels), jnp.float32)
    rim = jax.ShapeDtypeStruct((RIM, waves, spaxels), jnp.float32)
    half_rim = jax.ShapeDtypeStruct((HALO_BLOCKS, waves, spaxels), jnp.float32)
    moment = jax.ShapeDtypeStruct((MOMENT_ROWS, spaxels), jnp.float32)
    moment_all = jax.ShapeDtypeStruct((devices, MOMENT_ROWS, spaxels), jnp.float32)
    params = pltpu.CompilerParams(vmem_limit_bytes=VMEM_LIMIT)
    upward = [(i, (i + 1) % tiles) for i in range(tiles)]
    downward = [(j, i) for i, j in upward]

    def swap(upper, lower):
        return lax.ppermute(upper, "tile", upward), lax.ppermute(lower, "tile", downward)

    chunks = CHUNKS if groups % CHUNKS == 0 else 1
    weights, held, upper, lower = pl.pallas_call(
        rhs_kernel,
        out_shape=(jax.ShapeDtypeStruct(weights.shape, weights.dtype), window, rim, rim),
        in_specs=smem(3) + [pl.BlockSpec(memory_space=pltpu.HBM)] * 2,
        out_specs=tuple(vmem(4)),
        scratch_shapes=[
            pltpu.VMEM(fibre_data.shape, fibre_data.dtype),
            pltpu.VMEM(fibre_data.shape, jnp.float32),
            pltpu.SemaphoreType.DMA((chunks,)),
            pltpu.SemaphoreType.DMA,
        ],
        compiler_params=params,
        name="rhs",
    )(
        place,
        live_count,
        index,
        pltpu.with_memory_space_constraint(fibre_data, pltpu.HBM),
        pltpu.with_memory_space_constraint(weights, pltpu.HBM),
    )
    moments = jnp.zeros(moment.shape, jnp.float32)
    vectors = []
    for power in range(3):
        final = power == 2
        upper, lower = swap(upper, lower)
        out_rim = half_rim if final else rim
        vector, held, upper, lower, moments = pl.pallas_call(
            functools.partial(step_kernel, tiles, power, final),
            out_shape=(window, window, out_rim, out_rim, moment_all if final else moment),
            in_specs=smem(3) + vmem(5),
            out_specs=tuple(vmem(5)),
            scratch_shapes=[
                pltpu.VMEM((EXTENT, 2 * waves, spaxels), jnp.bfloat16),
                pltpu.VMEM((groups, 2 * waves, fibres), jnp.bfloat16),
            ],
            compiler_params=params,
            name=f"step{power}",
        )(place, live_count, index, held, upper, lower, moments, weights)
        vectors.append(vector)
    upper, lower = swap(upper, lower)
    moments = lax.all_to_all(moments, ("tile", "wave"), 0, 0)
    out = jax.ShapeDtypeStruct((waves, BLOCKS_DEV, spaxels), jnp.float32)
    return pl.pallas_call(
        functools.partial(final_kernel, tiles),
        out_shape=(out, out),
        in_specs=smem(1) + vmem(7),
        out_specs=tuple(vmem(2)),
        scratch_shapes=[pltpu.VMEM((BLOCKS_DEV, waves, spaxels), jnp.float32)],
        compiler_params=params,
        name="combine",
    )(place, moments, *vectors, held, upper, lower)


def solution(mesh):
    in_specs = (
        P("wave", "tile", None),
        P("wave", "tile", None, None, None),
        P("wave", "tile", None),
        P("tile"),
    )
    out_specs = (P("wave", "tile", None), P("wave", "tile", None))
    return jax.shard_map(shards, mesh=mesh, in_specs=in_specs, out_specs=out_specs, check_vma=False)
```

```python
import functools

import jax
import jax.numpy as jnp
from jax import lax
from jax.experimental import pallas as pl
from jax.experimental.pallas import tpu as pltpu
from jax.sharding import PartitionSpec as P

HALO_BLOCKS = 4
BLOCKS_DEV = 16
EXTENT = BLOCKS_DEV + 2 * HALO_BLOCKS
RIM = 2 * HALO_BLOCKS
TIKHONOV = 0.5
CHUNKS = 2
SCALE_ROWS = 16
CODE_PEAK = 32768.0
CODE_FLOOR = 1e-33
MOMENT_ROWS = 8
VMEM_LIMIT = 24 * 1024 * 1024


def split(value):
    upper = value.astype(jnp.bfloat16)
    lower = (value - upper.astype(jnp.float32)).astype(jnp.bfloat16)
    return upper, lower


def halves_sum(value):
    half = value.shape[0] // 2
    return value[:half] + value[half:]


def scatter(spread, place_ref, index_ref, group, partial_ref):
    lanes = partial_ref.shape[2]
    first = place_ref[0] * BLOCKS_DEV - HALO_BLOCKS
    for slot in range(index_ref.shape[0]):
        block = index_ref[slot, group] - first
        partial_ref[block] += spread[:, slot * lanes : (slot + 1) * lanes]


def spread_of(image, weights):
    return lax.dot_general(
        image, weights, (((1,), (1,)), ((), ())), preferred_element_type=jnp.float32
    )


def folded(value, rows, combine):
    parts = [value[start : start + rows] for start in range(0, value.shape[0], rows)]
    return functools.reduce(combine, parts)


def repeated(value, rows):
    return jnp.concatenate([value] * (rows // value.shape[0]), axis=0)


def encode(partial_ref, start, rim_ref):
    waves = partial_ref.shape[1]
    width = (rim_ref.shape[0] - SCALE_ROWS) // waves
    scales = rim_ref.at[width * waves :]
    peak = None
    for block in range(width):
        size = folded(jnp.abs(partial_ref[start + block]), 8, jnp.maximum)
        peak = size if peak is None else jnp.maximum(peak, size)
    scales[...] = repeated(jnp.maximum(peak, CODE_FLOOR), SCALE_ROWS).astype(jnp.bfloat16)
    gain = repeated(CODE_PEAK / scales[...].astype(jnp.float32), waves)
    for block in range(width):
        value = partial_ref[start + block] * gain
        for _ in range(3):
            value = value * jnp.abs(value)
        rim_ref[block * waves : (block + 1) * waves] = value.astype(jnp.bfloat16)


def decode_add(rim_ref, target_ref, start):
    waves = target_ref.shape[1]
    width = (rim_ref.shape[0] - SCALE_ROWS) // waves
    scale = repeated(rim_ref[width * waves :].astype(jnp.float32) / CODE_PEAK, waves)
    for block in range(width):
        code = rim_ref[block * waves : (block + 1) * waves].astype(jnp.float32)
        root = jnp.sqrt(jnp.sqrt(jnp.sqrt(jnp.abs(code))))
        target_ref[start + block] += jnp.where(code < 0.0, -root, root) * scale


def rim_starts(place_ref, extent, rim_ref, waves):
    top = extent - (rim_ref.shape[0] - SCALE_ROWS) // waves
    is_even = lax.rem(place_ref[0], 2) == 0
    return jnp.where(is_even, top, 0), jnp.where(is_even, 0, top)


def emit_rims(place_ref, partial_ref, even_ref, odd_ref):
    even, odd = rim_starts(place_ref, partial_ref.shape[0], even_ref, partial_ref.shape[1])
    encode(partial_ref, even, even_ref)
    encode(partial_ref, odd, odd_ref)


def add_rims(place_ref, target_ref, even_in_ref, odd_in_ref):
    even, odd = rim_starts(place_ref, target_ref.shape[0], even_in_ref, target_ref.shape[1])
    decode_add(even_in_ref, target_ref, even)
    decode_add(odd_in_ref, target_ref, odd)


def rhs_kernel(
    place_ref,
    live_ref,
    index_ref,
    data_ref,
    source_ref,
    kernels_ref,
    partial_ref,
    even_ref,
    odd_ref,
    narrow_ref,
    wide_ref,
    sems,
    data_sem,
):
    groups, slots, spaxels, fibres = kernels_ref.shape
    chunks = sems.shape[0]
    size = groups // chunks

    def copy(chunk):
        part = pl.ds(chunk * size, size)
        return pltpu.make_async_copy(source_ref.at[part], kernels_ref.at[part], sems.at[chunk])

    data_copy = pltpu.make_async_copy(data_ref, narrow_ref, data_sem)
    data_copy.start()
    for chunk in range(chunks):
        copy(chunk).start()
    partial_ref[...] = jnp.zeros_like(partial_ref)
    data_copy.wait()
    wide_ref[...] = narrow_ref[...].astype(jnp.float32)
    live = live_ref[0]
    for chunk in range(chunks):
        copy(chunk).wait()
        for group in range(chunk * size, (chunk + 1) * size):
            data = jnp.where(group < live, wide_ref[:, group, :], 0.0).astype(jnp.bfloat16)
            spread = spread_of(data, kernels_ref[group].reshape(slots * spaxels, fibres))
            scatter(spread, place_ref, index_ref, group, partial_ref)
    emit_rims(place_ref, partial_ref, even_ref, odd_ref)


def step_kernel(
    power,
    final,
    place_ref,
    live_ref,
    index_ref,
    held_ref,
    even_in_ref,
    odd_in_ref,
    moments_in_ref,
    kernels_ref,
    vector_ref,
    partial_ref,
    even_ref,
    odd_ref,
    moments_ref,
    operand_ref,
    image_ref,
):
    groups, slots, spaxels, fibres = kernels_ref.shape
    waves = held_ref.shape[1]
    live = live_ref[0]
    first_block = place_ref[0] * BLOCKS_DEV - HALO_BLOCKS
    vector_ref[...] = held_ref[...]
    add_rims(place_ref, vector_ref, even_in_ref, odd_in_ref)
    square = jnp.zeros(vector_ref.shape[1:], jnp.float32)
    for block in range(EXTENT):
        value = vector_ref[block]
        operand_ref[block, :waves], operand_ref[block, waves:] = split(value)
        if HALO_BLOCKS <= block < HALO_BLOCKS + BLOCKS_DEV:
            square = square + value * value
    partial_ref[...] = jnp.zeros_like(partial_ref)
    energy = jnp.zeros((waves, fibres), jnp.float32)
    for group in range(groups):
        picked = jnp.concatenate(
            [operand_ref[index_ref[slot, group] - first_block] for slot in range(slots)], axis=1
        )
        weights = kernels_ref[group].reshape(slots * spaxels, fibres)
        image = halves_sum(jnp.dot(picked, weights, preferred_element_type=jnp.float32))
        image = jnp.where(group < live, image, 0.0)
        energy = energy + image * image
        image_ref[group, :waves], image_ref[group, waves:] = split(image)
    for group in range(groups):
        weights = kernels_ref[group].reshape(slots * spaxels, fibres)
        spread = halves_sum(spread_of(image_ref[group], weights))
        scatter(spread, place_ref, index_ref, group, partial_ref)
    emit_rims(place_ref, partial_ref, even_ref, odd_ref)
    for block in range(EXTENT):
        partial_ref[block] += TIKHONOV * vector_ref[block]
    square_row = jnp.sum(square, axis=0, keepdims=True)
    energy_row = jnp.sum(energy, axis=0, keepdims=True) + TIKHONOV * square_row
    rows = lax.broadcasted_iota(jnp.int32, moments_in_ref.shape, 0)
    moments = jnp.where(
        rows == 2 * power,
        square_row,
        jnp.where(rows == 2 * power + 1, energy_row, moments_in_ref[...]),
    )
    moments_ref[...] = jnp.broadcast_to(moments, moments_ref.shape) if final else moments


def coefficients(moments, steps):
    def inner(first, second, shift):
        total = 0.0
        for i, a in enumerate(first):
            for j, b in enumerate(second):
                if a is not None and b is not None:
                    total = total + a * b * moments[i + j + shift]
        return total

    one = jnp.ones_like(moments[0])
    residual, direction = [one], [one]
    answer = []
    current = inner(residual, residual, 0)
    for step in range(steps):
        size = current / inner(direction, direction, 1)
        answer = [
            size * d + (answer[i] if i < len(answer) else 0.0) for i, d in enumerate(direction)
        ]
        shifted = [0.0] + [-size * d for d in direction]
        residual = [
            s + (residual[i] if i < len(residual) else 0.0) for i, s in enumerate(shifted)
        ]
        if step + 1 < steps:
            following = inner(residual, residual, 0)
            ratio = following / current
            direction = [
                r + (ratio * direction[i] if i < len(direction) else 0.0)
                for i, r in enumerate(residual)
            ]
            current = following
    return answer, residual


def final_kernel(
    place_ref,
    moments_ref,
    first_ref,
    second_ref,
    third_ref,
    held_ref,
    even_in_ref,
    odd_in_ref,
    solution_ref,
    residual_ref,
    last_ref,
):
    sums = moments_ref[0]
    for source in range(1, moments_ref.shape[0]):
        sums = sums + moments_ref[source]
    sums = jnp.sum(sums, axis=1, keepdims=True)
    lanes = first_ref.shape[2]
    raw = [jnp.broadcast_to(sums[row : row + 1], (1, lanes)) for row in range(6)]
    unit = raw[0] / raw[1]
    scaled, factor = [], 1.0 / raw[0]
    for row in range(6):
        scaled.append(raw[row] * factor)
        factor = factor * unit
    answer, residual = coefficients(scaled, 3)
    power = jnp.ones_like(unit)
    answer_scaled, residual_scaled = [], []
    for row in range(4):
        residual_scaled.append(residual[row] * power)
        power = power * unit
        if row < 3:
            answer_scaled.append(answer[row] * power)
    last_ref[...] = held_ref[pl.ds(HALO_BLOCKS, BLOCKS_DEV)]
    add_rims(place_ref, last_ref, even_in_ref, odd_in_ref)
    for block in range(BLOCKS_DEV):
        first = first_ref[HALO_BLOCKS + block]
        second = second_ref[HALO_BLOCKS + block]
        third = third_ref[HALO_BLOCKS + block]
        last = last_ref[block]
        solution_ref[:, block, :] = (
            answer_scaled[0] * first + answer_scaled[1] * second + answer_scaled[2] * third
        )
        residual_ref[:, block, :] = (
            first
            + residual_scaled[1] * second
            + residual_scaled[2] * third
            + residual_scaled[3] * last
        )


def vmem(count):
    return [pl.BlockSpec(memory_space=pltpu.VMEM)] * count


def smem(count):
    return [pl.BlockSpec(memory_space=pltpu.SMEM)] * count


def shards(fibre_data, kernels, block_index, live_count):
    tiles, devices = lax.axis_size("tile"), lax.axis_size("tile") * lax.axis_size("wave")
    _, groups, slots, spaxels, fibres = kernels.shape
    waves = fibre_data.shape[0]
    place = lax.axis_index("tile").reshape(1)
    index = jnp.swapaxes(block_index, 1, 2).reshape(slots, groups)
    weights = kernels.reshape(groups, slots, spaxels, fibres)
    window = jax.ShapeDtypeStruct((EXTENT, waves, spaxels), jnp.float32)
    rim = jax.ShapeDtypeStruct((RIM * waves + SCALE_ROWS, spaxels), jnp.bfloat16)
    half_rim = jax.ShapeDtypeStruct((HALO_BLOCKS * waves + SCALE_ROWS, spaxels), jnp.bfloat16)
    moment = jax.ShapeDtypeStruct((MOMENT_ROWS, spaxels), jnp.float32)
    moment_all = jax.ShapeDtypeStruct((devices, MOMENT_ROWS, spaxels), jnp.float32)
    params = pltpu.CompilerParams(vmem_limit_bytes=VMEM_LIMIT)
    even_pairs = [(i, i ^ 1) for i in range(tiles) if (i ^ 1) < tiles]
    odd_pairs = [
        (i, j) for i in range(tiles) for j in [((i + 1) ^ 1) - 1] if 0 <= j < tiles
    ]

    def swap(even, odd):
        return lax.ppermute(even, "tile", even_pairs), lax.ppermute(odd, "tile", odd_pairs)

    chunks = CHUNKS if groups % CHUNKS == 0 else 1
    weights, held, even, odd = pl.pallas_call(
        rhs_kernel,
        out_shape=(jax.ShapeDtypeStruct(weights.shape, weights.dtype), window, rim, rim),
        in_specs=smem(3) + [pl.BlockSpec(memory_space=pltpu.HBM)] * 2,
        out_specs=tuple(vmem(4)),
        scratch_shapes=[
            pltpu.VMEM(fibre_data.shape, fibre_data.dtype),
            pltpu.VMEM(fibre_data.shape, jnp.float32),
            pltpu.SemaphoreType.DMA((chunks,)),
            pltpu.SemaphoreType.DMA,
        ],
        compiler_params=params,
        name="rhs",
    )(
        place,
        live_count,
        index,
        pltpu.with_memory_space_constraint(fibre_data, pltpu.HBM),
        pltpu.with_memory_space_constraint(weights, pltpu.HBM),
    )
    moments = jnp.zeros(moment.shape, jnp.float32)
    vectors = []
    for power in range(3):
        final = power == 2
        even, odd = swap(even, odd)
        out_rim = half_rim if final else rim
        vector, held, even, odd, moments = pl.pallas_call(
            functools.partial(step_kernel, power, final),
            out_shape=(window, window, out_rim, out_rim, moment_all if final else moment),
            in_specs=smem(3) + vmem(5),
            out_specs=tuple(vmem(5)),
            scratch_shapes=[
                pltpu.VMEM((EXTENT, 2 * waves, spaxels), jnp.bfloat16),
                pltpu.VMEM((groups, 2 * waves, fibres), jnp.bfloat16),
            ],
            compiler_params=params,
            name=f"step{power}",
        )(place, live_count, index, held, even, odd, moments, weights)
        vectors.append(vector)
    even, odd = swap(even, odd)
    moments = lax.all_to_all(moments, ("tile", "wave"), 0, 0)
    out = jax.ShapeDtypeStruct((waves, BLOCKS_DEV, spaxels), jnp.float32)
    return pl.pallas_call(
        final_kernel,
        out_shape=(out, out),
        in_specs=smem(1) + vmem(7),
        out_specs=tuple(vmem(2)),
        scratch_shapes=[pltpu.VMEM((BLOCKS_DEV, waves, spaxels), jnp.float32)],
        compiler_params=params,
        name="combine",
    )(place, moments, *vectors, held, even, odd)


def solution(mesh):
    in_specs = (
        P("wave", "tile", None),
        P("wave", "tile", None, None, None),
        P("wave", "tile", None),
        P("tile"),
    )
    out_specs = (P("wave", "tile", None), P("wave", "tile", None))
    return jax.shard_map(shards, mesh=mesh, in_specs=in_specs, out_specs=out_specs, check_vma=False)
```

```python
import functools

import jax
import jax.numpy as jnp
from jax import lax
from jax.experimental import pallas as pl
from jax.experimental.pallas import tpu as pltpu
from jax.sharding import PartitionSpec as P

HALO_BLOCKS = 4
BLOCKS_DEV = 16
EXTENT = BLOCKS_DEV + 2 * HALO_BLOCKS
RIM = 2 * HALO_BLOCKS
TIKHONOV = 0.5
CHUNKS = 2
SCALE_ROWS = 16
CODE_PEAK = 32768.0
CODE_FLOOR = 1e-33
MOMENT_ROWS = 8
VMEM_LIMIT = 24 * 1024 * 1024


def split(value):
    upper = value.astype(jnp.bfloat16)
    lower = (value - upper.astype(jnp.float32)).astype(jnp.bfloat16)
    return upper, lower


def halves_sum(value):
    half = value.shape[0] // 2
    return value[:half] + value[half:]


def scatter(spread, place_ref, index_ref, group, partial_ref):
    lanes = partial_ref.shape[2]
    first = place_ref[0] * BLOCKS_DEV - HALO_BLOCKS
    for slot in range(index_ref.shape[0]):
        block = index_ref[slot, group] - first
        partial_ref[block] += spread[:, slot * lanes : (slot + 1) * lanes]


def spread_of(image, weights):
    return lax.dot_general(
        image, weights, (((1,), (1,)), ((), ())), preferred_element_type=jnp.float32
    )


def folded(value, rows, combine):
    parts = [value[start : start + rows] for start in range(0, value.shape[0], rows)]
    return functools.reduce(combine, parts)


def repeated(value, rows):
    return jnp.concatenate([value] * (rows // value.shape[0]), axis=0)


def encode(partial_ref, start, rim_ref):
    waves = partial_ref.shape[1]
    width = (rim_ref.shape[0] - SCALE_ROWS) // waves
    scales = rim_ref.at[width * waves :]
    peak = None
    for block in range(width):
        size = folded(jnp.abs(partial_ref[start + block]), 8, jnp.maximum)
        peak = size if peak is None else jnp.maximum(peak, size)
    scales[...] = repeated(jnp.maximum(peak, CODE_FLOOR), SCALE_ROWS).astype(jnp.bfloat16)
    gain = repeated(CODE_PEAK / scales[...].astype(jnp.float32), waves)
    for block in range(width):
        value = partial_ref[start + block] * gain
        for _ in range(3):
            value = value * jnp.abs(value)
        rim_ref[block * waves : (block + 1) * waves] = value.astype(jnp.bfloat16)


def decode_add(rim_ref, target_ref, start):
    waves = target_ref.shape[1]
    width = (rim_ref.shape[0] - SCALE_ROWS) // waves
    scale = repeated(rim_ref[width * waves :].astype(jnp.float32) / CODE_PEAK, waves)
    for block in range(width):
        code = rim_ref[block * waves : (block + 1) * waves].astype(jnp.float32)
        root = jnp.sqrt(jnp.sqrt(jnp.sqrt(jnp.abs(code))))
        target_ref[start + block] += jnp.where(code < 0.0, -root, root) * scale


def rim_starts(place_ref, extent, rim_ref, waves):
    top = extent - (rim_ref.shape[0] - SCALE_ROWS) // waves
    is_even = lax.rem(place_ref[0], 2) == 0
    return jnp.where(is_even, top, 0), jnp.where(is_even, 0, top)


def emit_rims(place_ref, partial_ref, even_ref, odd_ref):
    even, odd = rim_starts(place_ref, partial_ref.shape[0], even_ref, partial_ref.shape[1])
    encode(partial_ref, even, even_ref)
    encode(partial_ref, odd, odd_ref)


def add_rims(place_ref, target_ref, even_in_ref, odd_in_ref):
    even, odd = rim_starts(place_ref, target_ref.shape[0], even_in_ref, target_ref.shape[1])
    decode_add(even_in_ref, target_ref, even)
    decode_add(odd_in_ref, target_ref, odd)


def rhs_kernel(
    place_ref,
    live_ref,
    index_ref,
    data_ref,
    source_ref,
    kernels_ref,
    partial_ref,
    odd_ref,
    even_ref,
    narrow_ref,
    wide_ref,
    sems,
    data_sem,
):
    groups, slots, spaxels, fibres = kernels_ref.shape
    chunks = sems.shape[0]
    size = groups // chunks

    def copy(chunk):
        part = pl.ds(chunk * size, size)
        return pltpu.make_async_copy(source_ref.at[part], kernels_ref.at[part], sems.at[chunk])

    data_copy = pltpu.make_async_copy(data_ref, narrow_ref, data_sem)
    data_copy.start()
    for chunk in range(chunks):
        copy(chunk).start()
    partial_ref[...] = jnp.zeros_like(partial_ref)
    data_copy.wait()
    wide_ref[...] = narrow_ref[...].astype(jnp.float32)
    live = live_ref[0]
    for chunk in range(chunks):
        copy(chunk).wait()
        for group in range(chunk * size, (chunk + 1) * size):
            data = jnp.where(group < live, wide_ref[:, group, :], 0.0).astype(jnp.bfloat16)
            spread = spread_of(data, kernels_ref[group].reshape(slots * spaxels, fibres))
            scatter(spread, place_ref, index_ref, group, partial_ref)
    emit_rims(place_ref, partial_ref, even_ref, odd_ref)


def step_kernel(
    power,
    final,
    place_ref,
    live_ref,
    index_ref,
    held_ref,
    odd_in_ref,
    even_in_ref,
    moments_in_ref,
    kernels_ref,
    vector_ref,
    partial_ref,
    odd_ref,
    even_ref,
    moments_ref,
    operand_ref,
    image_ref,
):
    groups, slots, spaxels, fibres = kernels_ref.shape
    waves = held_ref.shape[1]
    live = live_ref[0]
    first_block = place_ref[0] * BLOCKS_DEV - HALO_BLOCKS
    vector_ref[...] = held_ref[...]
    add_rims(place_ref, vector_ref, even_in_ref, odd_in_ref)
    square = jnp.zeros(vector_ref.shape[1:], jnp.float32)
    for block in range(EXTENT):
        value = vector_ref[block]
        operand_ref[block, :waves], operand_ref[block, waves:] = split(value)
        if HALO_BLOCKS <= block < HALO_BLOCKS + BLOCKS_DEV:
            square = square + value * value
    partial_ref[...] = jnp.zeros_like(partial_ref)
    energy = jnp.zeros((waves, fibres), jnp.float32)
    for group in range(groups):
        picked = jnp.concatenate(
            [operand_ref[index_ref[slot, group] - first_block] for slot in range(slots)], axis=1
        )
        weights = kernels_ref[group].reshape(slots * spaxels, fibres)
        image = halves_sum(jnp.dot(picked, weights, preferred_element_type=jnp.float32))
        image = jnp.where(group < live, image, 0.0)
        energy = energy + image * image
        image_ref[group, :waves], image_ref[group, waves:] = split(image)
    for group in range(groups):
        weights = kernels_ref[group].reshape(slots * spaxels, fibres)
        spread = halves_sum(spread_of(image_ref[group], weights))
        scatter(spread, place_ref, index_ref, group, partial_ref)
    emit_rims(place_ref, partial_ref, even_ref, odd_ref)
    for block in range(EXTENT):
        partial_ref[block] += TIKHONOV * vector_ref[block]
    square_row = jnp.sum(square, axis=0, keepdims=True)
    energy_row = jnp.sum(energy, axis=0, keepdims=True) + TIKHONOV * square_row
    rows = lax.broadcasted_iota(jnp.int32, moments_in_ref.shape, 0)
    moments = jnp.where(
        rows == 2 * power,
        square_row,
        jnp.where(rows == 2 * power + 1, energy_row, moments_in_ref[...]),
    )
    moments_ref[...] = jnp.broadcast_to(moments, moments_ref.shape) if final else moments


def coefficients(moments, steps):
    def inner(first, second, shift):
        total = 0.0
        for i, a in enumerate(first):
            for j, b in enumerate(second):
                if a is not None and b is not None:
                    total = total + a * b * moments[i + j + shift]
        return total

    one = jnp.ones_like(moments[0])
    residual, direction = [one], [one]
    answer = []
    current = inner(residual, residual, 0)
    for step in range(steps):
        size = current / inner(direction, direction, 1)
        answer = [
            size * d + (answer[i] if i < len(answer) else 0.0) for i, d in enumerate(direction)
        ]
        shifted = [0.0] + [-size * d for d in direction]
        residual = [
            s + (residual[i] if i < len(residual) else 0.0) for i, s in enumerate(shifted)
        ]
        if step + 1 < steps:
            following = inner(residual, residual, 0)
            ratio = following / current
            direction = [
                r + (ratio * direction[i] if i < len(direction) else 0.0)
                for i, r in enumerate(residual)
            ]
            current = following
    return answer, residual


def final_kernel(
    place_ref,
    moments_ref,
    first_ref,
    second_ref,
    third_ref,
    held_ref,
    odd_in_ref,
    even_in_ref,
    solution_ref,
    residual_ref,
    last_ref,
):
    sums = moments_ref[0]
    for source in range(1, moments_ref.shape[0]):
        sums = sums + moments_ref[source]
    sums = jnp.sum(sums, axis=1, keepdims=True)
    lanes = first_ref.shape[2]
    raw = [jnp.broadcast_to(sums[row : row + 1], (1, lanes)) for row in range(6)]
    unit = raw[0] / raw[1]
    scaled, factor = [], 1.0 / raw[0]
    for row in range(6):
        scaled.append(raw[row] * factor)
        factor = factor * unit
    answer, residual = coefficients(scaled, 3)
    power = jnp.ones_like(unit)
    answer_scaled, residual_scaled = [], []
    for row in range(4):
        residual_scaled.append(residual[row] * power)
        power = power * unit
        if row < 3:
            answer_scaled.append(answer[row] * power)
    last_ref[...] = held_ref[pl.ds(HALO_BLOCKS, BLOCKS_DEV)]
    add_rims(place_ref, last_ref, even_in_ref, odd_in_ref)
    for block in range(BLOCKS_DEV):
        first = first_ref[HALO_BLOCKS + block]
        second = second_ref[HALO_BLOCKS + block]
        third = third_ref[HALO_BLOCKS + block]
        last = last_ref[block]
        solution_ref[:, block, :] = (
            answer_scaled[0] * first + answer_scaled[1] * second + answer_scaled[2] * third
        )
        residual_ref[:, block, :] = (
            first
            + residual_scaled[1] * second
            + residual_scaled[2] * third
            + residual_scaled[3] * last
        )


def vmem(count):
    return [pl.BlockSpec(memory_space=pltpu.VMEM)] * count


def smem(count):
    return [pl.BlockSpec(memory_space=pltpu.SMEM)] * count


def shards(fibre_data, kernels, block_index, live_count):
    tiles, devices = lax.axis_size("tile"), lax.axis_size("tile") * lax.axis_size("wave")
    _, groups, slots, spaxels, fibres = kernels.shape
    waves = fibre_data.shape[0]
    place = lax.axis_index("tile").reshape(1)
    index = jnp.swapaxes(block_index, 1, 2).reshape(slots, groups)
    weights = kernels.reshape(groups, slots, spaxels, fibres)
    window = jax.ShapeDtypeStruct((EXTENT, waves, spaxels), jnp.float32)
    rim = jax.ShapeDtypeStruct((RIM * waves + SCALE_ROWS, spaxels), jnp.bfloat16)
    half_rim = jax.ShapeDtypeStruct((HALO_BLOCKS * waves + SCALE_ROWS, spaxels), jnp.bfloat16)
    moment = jax.ShapeDtypeStruct((MOMENT_ROWS, spaxels), jnp.float32)
    moment_all = jax.ShapeDtypeStruct((devices, MOMENT_ROWS, spaxels), jnp.float32)
    params = pltpu.CompilerParams(vmem_limit_bytes=VMEM_LIMIT)
    even_pairs = [(i, i ^ 1) for i in range(tiles) if (i ^ 1) < tiles]
    odd_pairs = [
        (i, j) for i in range(tiles) for j in [((i + 1) ^ 1) - 1] if 0 <= j < tiles
    ]

    def swap(odd, even):
        return lax.ppermute(odd, "tile", odd_pairs), lax.ppermute(even, "tile", even_pairs)

    chunks = CHUNKS if groups % CHUNKS == 0 else 1
    weights, held, odd, even = pl.pallas_call(
        rhs_kernel,
        out_shape=(jax.ShapeDtypeStruct(weights.shape, weights.dtype), window, rim, rim),
        in_specs=smem(3) + [pl.BlockSpec(memory_space=pltpu.HBM)] * 2,
        out_specs=tuple(vmem(4)),
        scratch_shapes=[
            pltpu.VMEM(fibre_data.shape, fibre_data.dtype),
            pltpu.VMEM(fibre_data.shape, jnp.float32),
            pltpu.SemaphoreType.DMA((chunks,)),
            pltpu.SemaphoreType.DMA,
        ],
        compiler_params=params,
        name="rhs",
    )(
        place,
        live_count,
        index,
        pltpu.with_memory_space_constraint(fibre_data, pltpu.HBM),
        pltpu.with_memory_space_constraint(weights, pltpu.HBM),
    )
    moments = jnp.zeros(moment.shape, jnp.float32)
    vectors = []
    for power in range(3):
        final = power == 2
        odd, even = swap(odd, even)
        out_rim = half_rim if final else rim
        vector, held, odd, even, moments = pl.pallas_call(
            functools.partial(step_kernel, power, final),
            out_shape=(window, window, out_rim, out_rim, moment_all if final else moment),
            in_specs=smem(3) + vmem(5),
            out_specs=tuple(vmem(5)),
            scratch_shapes=[
                pltpu.VMEM((EXTENT, 2 * waves, spaxels), jnp.bfloat16),
                pltpu.VMEM((groups, 2 * waves, fibres), jnp.bfloat16),
            ],
            compiler_params=params,
            name=f"step{power}",
        )(place, live_count, index, held, odd, even, moments, weights)
        vectors.append(vector)
    odd, even = swap(odd, even)
    moments = lax.all_to_all(moments, ("tile", "wave"), 0, 0)
    out = jax.ShapeDtypeStruct((waves, BLOCKS_DEV, spaxels), jnp.float32)
    return pl.pallas_call(
        final_kernel,
        out_shape=(out, out),
        in_specs=smem(1) + vmem(7),
        out_specs=tuple(vmem(2)),
        scratch_shapes=[pltpu.VMEM((BLOCKS_DEV, waves, spaxels), jnp.float32)],
        compiler_params=params,
        name="combine",
    )(place, moments, *vectors, held, odd, even)


def solution(mesh):
    in_specs = (
        P("wave", "tile", None),
        P("wave", "tile", None, None, None),
        P("wave", "tile", None),
        P("tile"),
    )
    out_specs = (P("wave", "tile", None), P("wave", "tile", None))
    return jax.shard_map(shards, mesh=mesh, in_specs=in_specs, out_specs=out_specs, check_vma=False)
```

```python
import functools

import jax
import jax.numpy as jnp
from jax import lax
from jax.experimental import pallas as pl
from jax.experimental.pallas import tpu as pltpu
from jax.sharding import PartitionSpec as P

HALO_BLOCKS = 4
BLOCKS_DEV = 16
EXTENT = BLOCKS_DEV + 2 * HALO_BLOCKS
RIM = 2 * HALO_BLOCKS
TIKHONOV = 0.5
CHUNKS = 2
SCALE_ROWS = 16
CODE_PEAK = 32768.0
CODE_FLOOR = 1e-33
MOMENT_ROWS = 8
VMEM_LIMIT = 24 * 1024 * 1024


def split(value):
    upper = value.astype(jnp.bfloat16)
    lower = (value - upper.astype(jnp.float32)).astype(jnp.bfloat16)
    return upper, lower


def halves_sum(value):
    half = value.shape[0] // 2
    return value[:half] + value[half:]


def scatter(spread, place_ref, index_ref, group, partial_ref):
    lanes = partial_ref.shape[2]
    first = place_ref[0] * BLOCKS_DEV - HALO_BLOCKS
    for slot in range(index_ref.shape[0]):
        block = index_ref[slot, group] - first
        partial_ref[block] += spread[:, slot * lanes : (slot + 1) * lanes]


def spread_of(image, weights):
    return lax.dot_general(
        image, weights, (((1,), (1,)), ((), ())), preferred_element_type=jnp.float32
    )


def folded(value, rows, combine):
    parts = [value[start : start + rows] for start in range(0, value.shape[0], rows)]
    return functools.reduce(combine, parts)


def repeated(value, rows):
    return jnp.concatenate([value] * (rows // value.shape[0]), axis=0)


def encode(partial_ref, start, rim_ref):
    waves = partial_ref.shape[1]
    width = (rim_ref.shape[0] - SCALE_ROWS) // waves
    scales = rim_ref.at[width * waves :]
    peak = None
    for block in range(width):
        size = folded(jnp.abs(partial_ref[start + block]), 8, jnp.maximum)
        peak = size if peak is None else jnp.maximum(peak, size)
    scales[...] = repeated(jnp.maximum(peak, CODE_FLOOR), SCALE_ROWS).astype(jnp.bfloat16)
    gain = repeated(CODE_PEAK / scales[...].astype(jnp.float32), waves)
    for block in range(width):
        value = partial_ref[start + block] * gain
        for _ in range(3):
            value = value * jnp.abs(value)
        rim_ref[block * waves : (block + 1) * waves] = value.astype(jnp.bfloat16)


def decode_add(rim_ref, present, target_ref, start):
    waves = target_ref.shape[1]
    width = (rim_ref.shape[0] - SCALE_ROWS) // waves
    scale = rim_ref[width * waves :].astype(jnp.float32) / CODE_PEAK
    scale = repeated(jnp.where(present, scale, 0.0), waves)
    for block in range(width):
        code = rim_ref[block * waves : (block + 1) * waves].astype(jnp.float32)
        root = jnp.sqrt(jnp.sqrt(jnp.sqrt(jnp.abs(code))))
        target_ref[start + block] += jnp.where(code < 0.0, -root, root) * scale


def rim_top(extent, rim_ref, waves):
    return extent - (rim_ref.shape[0] - SCALE_ROWS) // waves


def emit_rims(partial_ref, upper_ref, lower_ref):
    encode(partial_ref, rim_top(partial_ref.shape[0], upper_ref, partial_ref.shape[1]), upper_ref)
    encode(partial_ref, 0, lower_ref)


def add_rims(tiles, place_ref, target_ref, from_below_ref, from_above_ref):
    tile = place_ref[0]
    top = rim_top(target_ref.shape[0], from_above_ref, target_ref.shape[1])
    decode_add(from_below_ref, tile > 0, target_ref, 0)
    decode_add(from_above_ref, tile < tiles - 1, target_ref, top)


def rhs_kernel(
    place_ref,
    live_ref,
    index_ref,
    data_ref,
    source_ref,
    kernels_ref,
    partial_ref,
    upper_ref,
    lower_ref,
    narrow_ref,
    wide_ref,
    sems,
    data_sem,
):
    groups, slots, spaxels, fibres = kernels_ref.shape
    chunks = sems.shape[0]
    size = groups // chunks

    def copy(chunk):
        part = pl.ds(chunk * size, size)
        return pltpu.make_async_copy(source_ref.at[part], kernels_ref.at[part], sems.at[chunk])

    data_copy = pltpu.make_async_copy(data_ref, narrow_ref, data_sem)
    data_copy.start()
    for chunk in range(chunks):
        copy(chunk).start()
    partial_ref[...] = jnp.zeros_like(partial_ref)
    data_copy.wait()
    wide_ref[...] = narrow_ref[...].astype(jnp.float32)
    live = live_ref[0]
    for chunk in range(chunks):
        copy(chunk).wait()
        for group in range(chunk * size, (chunk + 1) * size):
            data = jnp.where(group < live, wide_ref[:, group, :], 0.0).astype(jnp.bfloat16)
            spread = spread_of(data, kernels_ref[group].reshape(slots * spaxels, fibres))
            scatter(spread, place_ref, index_ref, group, partial_ref)
    emit_rims(partial_ref, upper_ref, lower_ref)


def step_kernel(
    tiles,
    power,
    final,
    place_ref,
    live_ref,
    index_ref,
    held_ref,
    from_below_ref,
    from_above_ref,
    moments_in_ref,
    kernels_ref,
    vector_ref,
    partial_ref,
    upper_ref,
    lower_ref,
    moments_ref,
    operand_ref,
    image_ref,
):
    groups, slots, spaxels, fibres = kernels_ref.shape
    waves = held_ref.shape[1]
    live = live_ref[0]
    first_block = place_ref[0] * BLOCKS_DEV - HALO_BLOCKS
    vector_ref[...] = held_ref[...]
    add_rims(tiles, place_ref, vector_ref, from_below_ref, from_above_ref)
    square = jnp.zeros(vector_ref.shape[1:], jnp.float32)
    for block in range(EXTENT):
        value = vector_ref[block]
        operand_ref[block, :waves], operand_ref[block, waves:] = split(value)
        if HALO_BLOCKS <= block < HALO_BLOCKS + BLOCKS_DEV:
            square = square + value * value
    partial_ref[...] = jnp.zeros_like(partial_ref)
    energy = jnp.zeros((waves, fibres), jnp.float32)
    for group in range(groups):
        picked = jnp.concatenate(
            [operand_ref[index_ref[slot, group] - first_block] for slot in range(slots)], axis=1
        )
        weights = kernels_ref[group].reshape(slots * spaxels, fibres)
        image = halves_sum(jnp.dot(picked, weights, preferred_element_type=jnp.float32))
        image = jnp.where(group < live, image, 0.0)
        energy = energy + image * image
        image_ref[group, :waves], image_ref[group, waves:] = split(image)
    for group in range(groups):
        weights = kernels_ref[group].reshape(slots * spaxels, fibres)
        spread = halves_sum(spread_of(image_ref[group], weights))
        scatter(spread, place_ref, index_ref, group, partial_ref)
    emit_rims(partial_ref, upper_ref, lower_ref)
    for block in range(EXTENT):
        partial_ref[block] += TIKHONOV * vector_ref[block]
    square_row = jnp.sum(square, axis=0, keepdims=True)
    energy_row = jnp.sum(energy, axis=0, keepdims=True) + TIKHONOV * square_row
    rows = lax.broadcasted_iota(jnp.int32, moments_in_ref.shape, 0)
    moments = jnp.where(
        rows == 2 * power,
        square_row,
        jnp.where(rows == 2 * power + 1, energy_row, moments_in_ref[...]),
    )
    moments_ref[...] = jnp.broadcast_to(moments, moments_ref.shape) if final else moments


def coefficients(moments, steps):
    def inner(first, second, shift):
        total = 0.0
        for i, a in enumerate(first):
            for j, b in enumerate(second):
                if a is not None and b is not None:
                    total = total + a * b * moments[i + j + shift]
        return total

    one = jnp.ones_like(moments[0])
    residual, direction = [one], [one]
    answer = []
    current = inner(residual, residual, 0)
    for step in range(steps):
        size = current / inner(direction, direction, 1)
        answer = [
            size * d + (answer[i] if i < len(answer) else 0.0) for i, d in enumerate(direction)
        ]
        shifted = [0.0] + [-size * d for d in direction]
        residual = [
            s + (residual[i] if i < len(residual) else 0.0) for i, s in enumerate(shifted)
        ]
        if step + 1 < steps:
            following = inner(residual, residual, 0)
            ratio = following / current
            direction = [
                r + (ratio * direction[i] if i < len(direction) else 0.0)
                for i, r in enumerate(residual)
            ]
            current = following
    return answer, residual


def final_kernel(
    tiles,
    place_ref,
    moments_ref,
    first_ref,
    second_ref,
    third_ref,
    held_ref,
    from_below_ref,
    from_above_ref,
    solution_ref,
    residual_ref,
    last_ref,
):
    sums = moments_ref[0]
    for source in range(1, moments_ref.shape[0]):
        sums = sums + moments_ref[source]
    sums = jnp.sum(sums, axis=1, keepdims=True)
    lanes = first_ref.shape[2]
    raw = [jnp.broadcast_to(sums[row : row + 1], (1, lanes)) for row in range(6)]
    unit = raw[0] / raw[1]
    scaled, factor = [], 1.0 / raw[0]
    for row in range(6):
        scaled.append(raw[row] * factor)
        factor = factor * unit
    answer, residual = coefficients(scaled, 3)
    power = jnp.ones_like(unit)
    answer_scaled, residual_scaled = [], []
    for row in range(4):
        residual_scaled.append(residual[row] * power)
        power = power * unit
        if row < 3:
            answer_scaled.append(answer[row] * power)
    last_ref[...] = held_ref[pl.ds(HALO_BLOCKS, BLOCKS_DEV)]
    add_rims(tiles, place_ref, last_ref, from_below_ref, from_above_ref)
    for block in range(BLOCKS_DEV):
        first = first_ref[HALO_BLOCKS + block]
        second = second_ref[HALO_BLOCKS + block]
        third = third_ref[HALO_BLOCKS + block]
        last = last_ref[block]
        solution_ref[:, block, :] = (
            answer_scaled[0] * first + answer_scaled[1] * second + answer_scaled[2] * third
        )
        residual_ref[:, block, :] = (
            first
            + residual_scaled[1] * second
            + residual_scaled[2] * third
            + residual_scaled[3] * last
        )


def vmem(count):
    return [pl.BlockSpec(memory_space=pltpu.VMEM)] * count


def smem(count):
    return [pl.BlockSpec(memory_space=pltpu.SMEM)] * count


def shards(fibre_data, kernels, block_index, live_count):
    tiles, devices = lax.axis_size("tile"), lax.axis_size("tile") * lax.axis_size("wave")
    _, groups, slots, spaxels, fibres = kernels.shape
    waves = fibre_data.shape[0]
    place = lax.axis_index("tile").reshape(1)
    index = jnp.swapaxes(block_index, 1, 2).reshape(slots, groups)
    weights = kernels.reshape(groups, slots, spaxels, fibres)
    window = jax.ShapeDtypeStruct((EXTENT, waves, spaxels), jnp.float32)
    rim = jax.ShapeDtypeStruct((RIM * waves + SCALE_ROWS, spaxels), jnp.bfloat16)
    half_rim = jax.ShapeDtypeStruct((HALO_BLOCKS * waves + SCALE_ROWS, spaxels), jnp.bfloat16)
    moment = jax.ShapeDtypeStruct((MOMENT_ROWS, spaxels), jnp.float32)
    moment_all = jax.ShapeDtypeStruct((devices, MOMENT_ROWS, spaxels), jnp.float32)
    params = pltpu.CompilerParams(vmem_limit_bytes=VMEM_LIMIT)
    upward = [(i, (i + 1) % tiles) for i in range(tiles)]
    downward = [(j, i) for i, j in upward]

    def swap(upper, lower):
        return lax.ppermute(upper, "tile", upward), lax.ppermute(lower, "tile", downward)

    chunks = CHUNKS if groups % CHUNKS == 0 else 1
    weights, held, upper, lower = pl.pallas_call(
        rhs_kernel,
        out_shape=(jax.ShapeDtypeStruct(weights.shape, weights.dtype), window, rim, rim),
        in_specs=smem(3) + [pl.BlockSpec(memory_space=pltpu.HBM)] * 2,
        out_specs=tuple(vmem(4)),
        scratch_shapes=[
            pltpu.VMEM(fibre_data.shape, fibre_data.dtype),
            pltpu.VMEM(fibre_data.shape, jnp.float32),
            pltpu.SemaphoreType.DMA((chunks,)),
            pltpu.SemaphoreType.DMA,
        ],
        compiler_params=params,
        name="rhs",
    )(
        place,
        live_count,
        index,
        pltpu.with_memory_space_constraint(fibre_data, pltpu.HBM),
        pltpu.with_memory_space_constraint(weights, pltpu.HBM),
    )
    moments = jnp.zeros(moment.shape, jnp.float32)
    vectors = []
    for power in range(3):
        final = power == 2
        upper, lower = swap(upper, lower)
        out_rim = half_rim if final else rim
        vector, held, upper, lower, moments = pl.pallas_call(
            functools.partial(step_kernel, tiles, power, final),
            out_shape=(window, window, out_rim, out_rim, moment_all if final else moment),
            in_specs=smem(3) + vmem(5),
            out_specs=tuple(vmem(5)),
            scratch_shapes=[
                pltpu.VMEM((EXTENT, 2 * waves, spaxels), jnp.bfloat16),
                pltpu.VMEM((groups, 2 * waves, fibres), jnp.bfloat16),
            ],
            compiler_params=params,
            name=f"step{power}",
        )(place, live_count, index, held, upper, lower, moments, weights)
        vectors.append(vector)
    upper, lower = swap(upper, lower)
    moments = lax.all_to_all(moments, ("tile", "wave"), 0, 0)
    out = jax.ShapeDtypeStruct((waves, BLOCKS_DEV, spaxels), jnp.float32)
    return pl.pallas_call(
        functools.partial(final_kernel, tiles),
        out_shape=(out, out),
        in_specs=smem(1) + vmem(7),
        out_specs=tuple(vmem(2)),
        scratch_shapes=[pltpu.VMEM((BLOCKS_DEV, waves, spaxels), jnp.float32)],
        compiler_params=params,
        name="combine",
    )(place, moments, *vectors, held, upper, lower)


def solution(mesh):
    in_specs = (
        P("wave", "tile", None),
        P("wave", "tile", None, None, None),
        P("wave", "tile", None),
        P("tile"),
    )
    out_specs = (P("wave", "tile", None), P("wave", "tile", None))
    return jax.shard_map(shards, mesh=mesh, in_specs=in_specs, out_specs=out_specs, check_vma=False)
```

```python
import functools

import jax
import jax.numpy as jnp
from jax import lax
from jax.experimental import pallas as pl
from jax.experimental.pallas import tpu as pltpu
from jax.sharding import PartitionSpec as P

HALO_BLOCKS = 4
BLOCKS_DEV = 16
EXTENT = BLOCKS_DEV + 2 * HALO_BLOCKS
RIM = 2 * HALO_BLOCKS
TIKHONOV = 0.5
CHUNKS = 2
SCALE_ROWS = 16
CODE_PEAK = 32768.0
CODE_FLOOR = 1e-33
MOMENT_ROWS = 8
VMEM_LIMIT = 24 * 1024 * 1024


def split(value):
    upper = value.astype(jnp.bfloat16)
    lower = (value - upper.astype(jnp.float32)).astype(jnp.bfloat16)
    return upper, lower


def halves_sum(value):
    half = value.shape[0] // 2
    return value[:half] + value[half:]


def scatter(spread, place_ref, index_ref, group, partial_ref):
    lanes = partial_ref.shape[2]
    first = place_ref[0] * BLOCKS_DEV - HALO_BLOCKS
    for slot in range(index_ref.shape[0]):
        block = index_ref[slot, group] - first
        partial_ref[block] += spread[:, slot * lanes : (slot + 1) * lanes]


def spread_of(image, weights):
    return lax.dot_general(
        image, weights, (((1,), (1,)), ((), ())), preferred_element_type=jnp.float32
    )


def folded(value, rows, combine):
    parts = [value[start : start + rows] for start in range(0, value.shape[0], rows)]
    return functools.reduce(combine, parts)


def repeated(value, rows):
    return jnp.concatenate([value] * (rows // value.shape[0]), axis=0)


def encode(partial_ref, start, rim_ref):
    waves = partial_ref.shape[1]
    width = (rim_ref.shape[0] - SCALE_ROWS) // waves
    scales = rim_ref.at[width * waves :]
    peak = None
    for block in range(width):
        size = folded(jnp.abs(partial_ref[start + block]), 8, jnp.maximum)
        peak = size if peak is None else jnp.maximum(peak, size)
    scales[...] = repeated(jnp.maximum(peak, CODE_FLOOR), SCALE_ROWS).astype(jnp.bfloat16)
    gain = repeated(CODE_PEAK / scales[...].astype(jnp.float32), waves)
    for block in range(width):
        value = partial_ref[start + block] * gain
        for _ in range(3):
            value = value * jnp.abs(value)
        rim_ref[block * waves : (block + 1) * waves] = value.astype(jnp.bfloat16)


def decode_add(rim_ref, present, target_ref, start):
    waves = target_ref.shape[1]
    width = (rim_ref.shape[0] - SCALE_ROWS) // waves
    scale = rim_ref[width * waves :].astype(jnp.float32) / CODE_PEAK
    scale = repeated(jnp.where(present, scale, 0.0), waves)
    for block in range(width):
        code = rim_ref[block * waves : (block + 1) * waves].astype(jnp.float32)
        root = jnp.sqrt(jnp.sqrt(jnp.sqrt(jnp.abs(code))))
        target_ref[start + block] += jnp.where(code < 0.0, -root, root) * scale


def rim_top(extent, rim_ref, waves):
    return extent - (rim_ref.shape[0] - SCALE_ROWS) // waves


def rim_start(place_ref, extent, rim_ref, waves, upper):
    return jnp.where(upper == (place_ref[1] == 0), rim_top(extent, rim_ref, waves), 0)


def emit_rims(place_ref, partial_ref, onward_ref, return_ref):
    extent, waves = partial_ref.shape[:2]
    for upper, rim_ref in ((True, onward_ref), (False, return_ref)):
        encode(partial_ref, rim_start(place_ref, extent, rim_ref, waves, upper), rim_ref)


def add_rims(tiles, place_ref, target_ref, onward_in_ref, return_in_ref):
    extent, waves = target_ref.shape[:2]
    for upper, rim_ref in ((False, onward_in_ref), (True, return_in_ref)):
        start = rim_start(place_ref, extent, rim_ref, waves, upper)
        end_tile = jnp.where(start > 0, tiles - 1, 0)
        decode_add(rim_ref, place_ref[0] != end_tile, target_ref, start)


def rhs_kernel(
    place_ref,
    live_ref,
    index_ref,
    data_ref,
    source_ref,
    kernels_ref,
    partial_ref,
    onward_ref,
    return_ref,
    narrow_ref,
    wide_ref,
    sems,
    data_sem,
):
    groups, slots, spaxels, fibres = kernels_ref.shape
    chunks = sems.shape[0]
    size = groups // chunks

    def copy(chunk):
        part = pl.ds(chunk * size, size)
        return pltpu.make_async_copy(source_ref.at[part], kernels_ref.at[part], sems.at[chunk])

    data_copy = pltpu.make_async_copy(data_ref, narrow_ref, data_sem)
    data_copy.start()
    for chunk in range(chunks):
        copy(chunk).start()
    partial_ref[...] = jnp.zeros_like(partial_ref)
    data_copy.wait()
    wide_ref[...] = narrow_ref[...].astype(jnp.float32)
    live = live_ref[0]
    for chunk in range(chunks):
        copy(chunk).wait()
        for group in range(chunk * size, (chunk + 1) * size):
            data = jnp.where(group < live, wide_ref[:, group, :], 0.0).astype(jnp.bfloat16)
            spread = spread_of(data, kernels_ref[group].reshape(slots * spaxels, fibres))
            scatter(spread, place_ref, index_ref, group, partial_ref)
    emit_rims(place_ref, partial_ref, onward_ref, return_ref)


def step_kernel(
    tiles,
    power,
    final,
    place_ref,
    live_ref,
    index_ref,
    held_ref,
    onward_in_ref,
    return_in_ref,
    moments_in_ref,
    kernels_ref,
    vector_ref,
    partial_ref,
    onward_ref,
    return_ref,
    moments_ref,
    operand_ref,
    image_ref,
):
    groups, slots, spaxels, fibres = kernels_ref.shape
    waves = held_ref.shape[1]
    live = live_ref[0]
    first_block = place_ref[0] * BLOCKS_DEV - HALO_BLOCKS
    vector_ref[...] = held_ref[...]
    add_rims(tiles, place_ref, vector_ref, onward_in_ref, return_in_ref)
    square = jnp.zeros(vector_ref.shape[1:], jnp.float32)
    for block in range(EXTENT):
        value = vector_ref[block]
        operand_ref[block, :waves], operand_ref[block, waves:] = split(value)
        if HALO_BLOCKS <= block < HALO_BLOCKS + BLOCKS_DEV:
            square = square + value * value
    partial_ref[...] = jnp.zeros_like(partial_ref)
    energy = jnp.zeros((waves, fibres), jnp.float32)
    for group in range(groups):
        picked = jnp.concatenate(
            [operand_ref[index_ref[slot, group] - first_block] for slot in range(slots)], axis=1
        )
        weights = kernels_ref[group].reshape(slots * spaxels, fibres)
        image = halves_sum(jnp.dot(picked, weights, preferred_element_type=jnp.float32))
        image = jnp.where(group < live, image, 0.0)
        energy = energy + image * image
        image_ref[group, :waves], image_ref[group, waves:] = split(image)
    for group in range(groups):
        weights = kernels_ref[group].reshape(slots * spaxels, fibres)
        spread = halves_sum(spread_of(image_ref[group], weights))
        scatter(spread, place_ref, index_ref, group, partial_ref)
    emit_rims(place_ref, partial_ref, onward_ref, return_ref)
    for block in range(EXTENT):
        partial_ref[block] += TIKHONOV * vector_ref[block]
    square_row = jnp.sum(square, axis=0, keepdims=True)
    energy_row = jnp.sum(energy, axis=0, keepdims=True) + TIKHONOV * square_row
    rows = lax.broadcasted_iota(jnp.int32, moments_in_ref.shape, 0)
    moments = jnp.where(
        rows == 2 * power,
        square_row,
        jnp.where(rows == 2 * power + 1, energy_row, moments_in_ref[...]),
    )
    moments_ref[...] = jnp.broadcast_to(moments, moments_ref.shape) if final else moments


def coefficients(moments, steps):
    def inner(first, second, shift):
        total = 0.0
        for i, a in enumerate(first):
            for j, b in enumerate(second):
                if a is not None and b is not None:
                    total = total + a * b * moments[i + j + shift]
        return total

    one = jnp.ones_like(moments[0])
    residual, direction = [one], [one]
    answer = []
    current = inner(residual, residual, 0)
    for step in range(steps):
        size = current / inner(direction, direction, 1)
        answer = [
            size * d + (answer[i] if i < len(answer) else 0.0) for i, d in enumerate(direction)
        ]
        shifted = [0.0] + [-size * d for d in direction]
        residual = [
            s + (residual[i] if i < len(residual) else 0.0) for i, s in enumerate(shifted)
        ]
        if step + 1 < steps:
            following = inner(residual, residual, 0)
            ratio = following / current
            direction = [
                r + (ratio * direction[i] if i < len(direction) else 0.0)
                for i, r in enumerate(residual)
            ]
            current = following
    return answer, residual


def final_kernel(
    tiles,
    place_ref,
    moments_ref,
    first_ref,
    second_ref,
    third_ref,
    held_ref,
    onward_in_ref,
    return_in_ref,
    solution_ref,
    residual_ref,
    last_ref,
):
    sums = moments_ref[0]
    for source in range(1, moments_ref.shape[0]):
        sums = sums + moments_ref[source]
    sums = jnp.sum(sums, axis=1, keepdims=True)
    lanes = first_ref.shape[2]
    raw = [jnp.broadcast_to(sums[row : row + 1], (1, lanes)) for row in range(6)]
    unit = raw[0] / raw[1]
    scaled, factor = [], 1.0 / raw[0]
    for row in range(6):
        scaled.append(raw[row] * factor)
        factor = factor * unit
    answer, residual = coefficients(scaled, 3)
    power = jnp.ones_like(unit)
    answer_scaled, residual_scaled = [], []
    for row in range(4):
        residual_scaled.append(residual[row] * power)
        power = power * unit
        if row < 3:
            answer_scaled.append(answer[row] * power)
    last_ref[...] = held_ref[pl.ds(HALO_BLOCKS, BLOCKS_DEV)]
    add_rims(tiles, place_ref, last_ref, onward_in_ref, return_in_ref)
    for block in range(BLOCKS_DEV):
        first = first_ref[HALO_BLOCKS + block]
        second = second_ref[HALO_BLOCKS + block]
        third = third_ref[HALO_BLOCKS + block]
        last = last_ref[block]
        solution_ref[:, block, :] = (
            answer_scaled[0] * first + answer_scaled[1] * second + answer_scaled[2] * third
        )
        residual_ref[:, block, :] = (
            first
            + residual_scaled[1] * second
            + residual_scaled[2] * third
            + residual_scaled[3] * last
        )


def vmem(count):
    return [pl.BlockSpec(memory_space=pltpu.VMEM)] * count


def smem(count):
    return [pl.BlockSpec(memory_space=pltpu.SMEM)] * count


def circuit_of(tiles, waves):
    pairs = []
    for wave in range(0, waves, 2):
        path = [tile * waves + wave for tile in range(tiles)]
        if wave + 1 < waves:
            path += [tile * waves + wave + 1 for tile in reversed(range(tiles))]
        pairs += [(node, path[(step + 1) % len(path)]) for step, node in enumerate(path)]
    return pairs


def shards(fibre_data, kernels, block_index, live_count):
    tiles, devices = lax.axis_size("tile"), lax.axis_size("tile") * lax.axis_size("wave")
    _, groups, slots, spaxels, fibres = kernels.shape
    waves = fibre_data.shape[0]
    place = jnp.stack([lax.axis_index("tile"), lax.axis_index("wave") % 2])
    index = jnp.swapaxes(block_index, 1, 2).reshape(slots, groups)
    weights = kernels.reshape(groups, slots, spaxels, fibres)
    window = jax.ShapeDtypeStruct((EXTENT, waves, spaxels), jnp.float32)
    rim = jax.ShapeDtypeStruct((RIM * waves + SCALE_ROWS, spaxels), jnp.bfloat16)
    half_rim = jax.ShapeDtypeStruct((HALO_BLOCKS * waves + SCALE_ROWS, spaxels), jnp.bfloat16)
    moment = jax.ShapeDtypeStruct((MOMENT_ROWS, spaxels), jnp.float32)
    moment_all = jax.ShapeDtypeStruct((devices, MOMENT_ROWS, spaxels), jnp.float32)
    params = pltpu.CompilerParams(vmem_limit_bytes=VMEM_LIMIT)
    circuit = circuit_of(tiles, lax.axis_size("wave"))
    reverse = [(j, i) for i, j in circuit]

    def swap(onward, back):
        axes = ("tile", "wave")
        return lax.ppermute(onward, axes, circuit), lax.ppermute(back, axes, reverse)

    chunks = CHUNKS if groups % CHUNKS == 0 else 1
    weights, held, onward, back = pl.pallas_call(
        rhs_kernel,
        out_shape=(jax.ShapeDtypeStruct(weights.shape, weights.dtype), window, rim, rim),
        in_specs=smem(3) + [pl.BlockSpec(memory_space=pltpu.HBM)] * 2,
        out_specs=tuple(vmem(4)),
        scratch_shapes=[
            pltpu.VMEM(fibre_data.shape, fibre_data.dtype),
            pltpu.VMEM(fibre_data.shape, jnp.float32),
            pltpu.SemaphoreType.DMA((chunks,)),
            pltpu.SemaphoreType.DMA,
        ],
        compiler_params=params,
        name="rhs",
    )(
        place,
        live_count,
        index,
        pltpu.with_memory_space_constraint(fibre_data, pltpu.HBM),
        pltpu.with_memory_space_constraint(weights, pltpu.HBM),
    )
    moments = jnp.zeros(moment.shape, jnp.float32)
    vectors = []
    for power in range(3):
        final = power == 2
        onward, back = swap(onward, back)
        out_rim = half_rim if final else rim
        vector, held, onward, back, moments = pl.pallas_call(
            functools.partial(step_kernel, tiles, power, final),
            out_shape=(window, window, out_rim, out_rim, moment_all if final else moment),
            in_specs=smem(3) + vmem(5),
            out_specs=tuple(vmem(5)),
            scratch_shapes=[
                pltpu.VMEM((EXTENT, 2 * waves, spaxels), jnp.bfloat16),
                pltpu.VMEM((groups, 2 * waves, fibres), jnp.bfloat16),
            ],
            compiler_params=params,
            name=f"step{power}",
        )(place, live_count, index, held, onward, back, moments, weights)
        vectors.append(vector)
    onward, back = swap(onward, back)
    moments = lax.all_to_all(moments, ("tile", "wave"), 0, 0)
    out = jax.ShapeDtypeStruct((waves, BLOCKS_DEV, spaxels), jnp.float32)
    return pl.pallas_call(
        functools.partial(final_kernel, tiles),
        out_shape=(out, out),
        in_specs=smem(1) + vmem(7),
        out_specs=tuple(vmem(2)),
        scratch_shapes=[pltpu.VMEM((BLOCKS_DEV, waves, spaxels), jnp.float32)],
        compiler_params=params,
        name="combine",
    )(place, moments, *vectors, held, onward, back)


def solution(mesh):
    in_specs = (
        P("wave", "tile", None),
        P("wave", "tile", None, None, None),
        P("wave", "tile", None),
        P("tile"),
    )
    out_specs = (P("wave", "tile", None), P("wave", "tile", None))
    return jax.shard_map(shards, mesh=mesh, in_specs=in_specs, out_specs=out_specs, check_vma=False)
```

```python
import functools

import jax
import jax.numpy as jnp
from jax import lax
from jax.experimental import pallas as pl
from jax.experimental.pallas import tpu as pltpu
from jax.sharding import PartitionSpec as P

HALO_BLOCKS = 4
BLOCKS_DEV = 16
EXTENT = BLOCKS_DEV + 2 * HALO_BLOCKS
RIM = 2 * HALO_BLOCKS
TIKHONOV = 0.5
ITERATIONS = 3
SPREAD_LIMIT = 40.0
CHUNKS = 2
SCALE_ROWS = 16
CODE_PEAK = 32768.0
CODE_FLOOR = 1e-33
MOMENT_ROWS = 8
VMEM_LIMIT = 24 * 1024 * 1024


def split(value):
    upper = value.astype(jnp.bfloat16)
    lower = (value - upper.astype(jnp.float32)).astype(jnp.bfloat16)
    return upper, lower


def halves_sum(value):
    half = value.shape[0] // 2
    return value[:half] + value[half:]


def scatter(spread, place_ref, index_ref, group, partial_ref):
    lanes = partial_ref.shape[2]
    first = place_ref[0] * BLOCKS_DEV - HALO_BLOCKS
    for slot in range(index_ref.shape[0]):
        block = index_ref[slot, group] - first
        partial_ref[block] += spread[:, slot * lanes : (slot + 1) * lanes]


def spread_of(image, weights):
    return lax.dot_general(
        image, weights, (((1,), (1,)), ((), ())), preferred_element_type=jnp.float32
    )


def folded(value, rows, combine):
    parts = [value[start : start + rows] for start in range(0, value.shape[0], rows)]
    return functools.reduce(combine, parts)


def repeated(value, rows):
    return jnp.concatenate([value] * (rows // value.shape[0]), axis=0)


def encode(partial_ref, start, rim_ref):
    waves = partial_ref.shape[1]
    width = (rim_ref.shape[0] - SCALE_ROWS) // waves
    scales = rim_ref.at[width * waves :]
    peak = None
    for block in range(width):
        size = folded(jnp.abs(partial_ref[start + block]), 8, jnp.maximum)
        peak = size if peak is None else jnp.maximum(peak, size)
    scales[...] = repeated(jnp.maximum(peak, CODE_FLOOR), SCALE_ROWS).astype(jnp.bfloat16)
    gain = repeated(CODE_PEAK / scales[...].astype(jnp.float32), waves)
    for block in range(width):
        value = partial_ref[start + block] * gain
        for _ in range(3):
            value = value * jnp.abs(value)
        rim_ref[block * waves : (block + 1) * waves] = value.astype(jnp.bfloat16)


def decode_add(rim_ref, present, target_ref, start):
    waves = target_ref.shape[1]
    width = (rim_ref.shape[0] - SCALE_ROWS) // waves
    scale = rim_ref[width * waves :].astype(jnp.float32) / CODE_PEAK
    scale = repeated(jnp.where(present, scale, 0.0), waves)
    for block in range(width):
        code = rim_ref[block * waves : (block + 1) * waves].astype(jnp.float32)
        root = jnp.sqrt(jnp.sqrt(jnp.sqrt(jnp.abs(code))))
        target_ref[start + block] += jnp.where(code < 0.0, -root, root) * scale


def rim_top(extent, rim_ref, waves):
    return extent - (rim_ref.shape[0] - SCALE_ROWS) // waves


def rim_start(lane_ref, extent, rim_ref, waves, upper):
    return jnp.where(upper == (lane_ref[0] == 0), rim_top(extent, rim_ref, waves), 0)


def emit_rims(lane_ref, partial_ref, onward_ref, return_ref):
    extent, waves = partial_ref.shape[:2]
    for upper, rim_ref in ((True, onward_ref), (False, return_ref)):
        encode(partial_ref, rim_start(lane_ref, extent, rim_ref, waves, upper), rim_ref)


def add_rims(tiles, place_ref, lane_ref, target_ref, onward_in_ref, return_in_ref):
    extent, waves = target_ref.shape[:2]
    for upper, rim_ref in ((False, onward_in_ref), (True, return_in_ref)):
        start = rim_start(lane_ref, extent, rim_ref, waves, upper)
        end_tile = jnp.where(start > 0, tiles - 1, 0)
        decode_add(rim_ref, place_ref[0] != end_tile, target_ref, start)


def rhs_kernel(
    place_ref,
    lane_ref,
    live_ref,
    index_ref,
    data_ref,
    source_ref,
    kernels_ref,
    partial_ref,
    onward_ref,
    return_ref,
    narrow_ref,
    wide_ref,
    sems,
    data_sem,
):
    groups, slots, spaxels, fibres = kernels_ref.shape
    chunks = sems.shape[0]
    size = groups // chunks

    def copy(chunk):
        part = pl.ds(chunk * size, size)
        return pltpu.make_async_copy(source_ref.at[part], kernels_ref.at[part], sems.at[chunk])

    data_copy = pltpu.make_async_copy(data_ref, narrow_ref, data_sem)
    data_copy.start()
    for chunk in range(chunks):
        copy(chunk).start()
    partial_ref[...] = jnp.zeros_like(partial_ref)
    data_copy.wait()
    wide_ref[...] = narrow_ref[...].astype(jnp.float32)
    live = live_ref[0]
    for chunk in range(chunks):
        copy(chunk).wait()
        for group in range(chunk * size, (chunk + 1) * size):
            data = jnp.where(group < live, wide_ref[:, group, :], 0.0).astype(jnp.bfloat16)
            spread = spread_of(data, kernels_ref[group].reshape(slots * spaxels, fibres))
            scatter(spread, place_ref, index_ref, group, partial_ref)
    emit_rims(lane_ref, partial_ref, onward_ref, return_ref)


def step_kernel(
    tiles,
    power,
    final,
    place_ref,
    lane_ref,
    live_ref,
    index_ref,
    held_ref,
    onward_in_ref,
    return_in_ref,
    moments_in_ref,
    kernels_ref,
    vector_ref,
    partial_ref,
    onward_ref,
    return_ref,
    moments_ref,
    operand_ref,
    image_ref,
):
    groups, slots, spaxels, fibres = kernels_ref.shape
    waves = held_ref.shape[1]
    live = live_ref[0]
    first_block = place_ref[0] * BLOCKS_DEV - HALO_BLOCKS
    vector_ref[...] = held_ref[...]
    add_rims(tiles, place_ref, lane_ref, vector_ref, onward_in_ref, return_in_ref)
    square = jnp.zeros(vector_ref.shape[1:], jnp.float32)
    for block in range(EXTENT):
        value = vector_ref[block]
        operand_ref[block, :waves], operand_ref[block, waves:] = split(value)
        if HALO_BLOCKS <= block < HALO_BLOCKS + BLOCKS_DEV:
            square = square + value * value
    partial_ref[...] = jnp.zeros_like(partial_ref)
    energy = jnp.zeros((waves, fibres), jnp.float32)
    for group in range(groups):
        picked = jnp.concatenate(
            [operand_ref[index_ref[slot, group] - first_block] for slot in range(slots)], axis=1
        )
        weights = kernels_ref[group].reshape(slots * spaxels, fibres)
        image = halves_sum(jnp.dot(picked, weights, preferred_element_type=jnp.float32))
        image = jnp.where(group < live, image, 0.0)
        energy = energy + image * image
        image_ref[group, :waves], image_ref[group, waves:] = split(image)
    for group in range(groups):
        weights = kernels_ref[group].reshape(slots * spaxels, fibres)
        spread = halves_sum(spread_of(image_ref[group], weights))
        scatter(spread, place_ref, index_ref, group, partial_ref)
    emit_rims(lane_ref, partial_ref, onward_ref, return_ref)
    for block in range(EXTENT):
        partial_ref[block] += TIKHONOV * vector_ref[block]
    square_row = jnp.sum(square, axis=0, keepdims=True)
    energy_row = jnp.sum(energy, axis=0, keepdims=True) + TIKHONOV * square_row
    rows = lax.broadcasted_iota(jnp.int32, moments_in_ref.shape, 0)
    moments = jnp.where(
        rows == 2 * power,
        square_row,
        jnp.where(rows == 2 * power + 1, energy_row, moments_in_ref[...]),
    )
    moments_ref[...] = jnp.broadcast_to(moments, moments_ref.shape) if final else moments


def coefficients(moments, steps):
    def inner(first, second, shift):
        total = 0.0
        for i, a in enumerate(first):
            for j, b in enumerate(second):
                if a is not None and b is not None:
                    total = total + a * b * moments[i + j + shift]
        return total

    one = jnp.ones_like(moments[0])
    residual, direction = [one], [one]
    answer = []
    current = inner(residual, residual, 0)
    for step in range(steps):
        size = current / inner(direction, direction, 1)
        answer = [
            size * d + (answer[i] if i < len(answer) else 0.0) for i, d in enumerate(direction)
        ]
        shifted = [0.0] + [-size * d for d in direction]
        residual = [
            s + (residual[i] if i < len(residual) else 0.0) for i, s in enumerate(shifted)
        ]
        if step + 1 < steps:
            following = inner(residual, residual, 0)
            ratio = following / current
            direction = [
                r + (ratio * direction[i] if i < len(direction) else 0.0)
                for i, r in enumerate(residual)
            ]
            current = following
    return answer, residual


def final_kernel(
    tiles,
    place_ref,
    lane_ref,
    moments_ref,
    first_ref,
    second_ref,
    third_ref,
    held_ref,
    onward_in_ref,
    return_in_ref,
    solution_ref,
    residual_ref,
    flag_ref,
    last_ref,
):
    sums = moments_ref[0]
    for source in range(1, moments_ref.shape[0]):
        sums = sums + moments_ref[source]
    sums = jnp.sum(sums, axis=1, keepdims=True)
    lanes = first_ref.shape[2]
    raw = [jnp.broadcast_to(sums[row : row + 1], (1, lanes)) for row in range(6)]
    unit = raw[0] / raw[1]
    scaled, factor = [], 1.0 / raw[0]
    for row in range(6):
        scaled.append(raw[row] * factor)
        factor = factor * unit
    answer, residual = coefficients(scaled, ITERATIONS)
    sizes = [jnp.sqrt(scaled[2 * row]) for row in range(3)]
    sizes.append(scaled[5] / sizes[2])
    terms = sum(jnp.abs(c) * size for c, size in zip(residual, sizes))
    flag_ref[0] = jnp.min(jnp.where(terms <= SPREAD_LIMIT, 1, 0))
    power = jnp.ones_like(unit)
    answer_scaled, residual_scaled = [], []
    for row in range(4):
        residual_scaled.append(residual[row] * power)
        power = power * unit
        if row < 3:
            answer_scaled.append(answer[row] * power)
    last_ref[...] = held_ref[pl.ds(HALO_BLOCKS, BLOCKS_DEV)]
    add_rims(tiles, place_ref, lane_ref, last_ref, onward_in_ref, return_in_ref)
    for block in range(BLOCKS_DEV):
        first = first_ref[HALO_BLOCKS + block]
        second = second_ref[HALO_BLOCKS + block]
        third = third_ref[HALO_BLOCKS + block]
        last = last_ref[block]
        solution_ref[:, block, :] = (
            answer_scaled[0] * first + answer_scaled[1] * second + answer_scaled[2] * third
        )
        residual_ref[:, block, :] = (
            first
            + residual_scaled[1] * second
            + residual_scaled[2] * third
            + residual_scaled[3] * last
        )


def vmem(count):
    return [pl.BlockSpec(memory_space=pltpu.VMEM)] * count


def smem(count):
    return [pl.BlockSpec(memory_space=pltpu.SMEM)] * count


def circuit_of(tiles, waves):
    pairs = []
    for wave in range(0, waves, 2):
        path = [tile * waves + wave for tile in range(tiles)]
        if wave + 1 < waves:
            path += [tile * waves + wave + 1 for tile in reversed(range(tiles))]
        pairs += [(node, path[(step + 1) % len(path)]) for step, node in enumerate(path)]
    return pairs


def shards(fibre_data, kernels, block_index, live_count):
    tiles, devices = lax.axis_size("tile"), lax.axis_size("tile") * lax.axis_size("wave")
    _, groups, slots, spaxels, fibres = kernels.shape
    waves = fibre_data.shape[0]
    place = lax.axis_index("tile").reshape(1)
    lane = (lax.axis_index("wave") % 2).reshape(1)
    index = jnp.swapaxes(block_index, 1, 2).reshape(slots, groups)
    weights = kernels.reshape(groups, slots, spaxels, fibres)
    window = jax.ShapeDtypeStruct((EXTENT, waves, spaxels), jnp.float32)
    rim = jax.ShapeDtypeStruct((RIM * waves + SCALE_ROWS, spaxels), jnp.bfloat16)
    half_rim = jax.ShapeDtypeStruct((HALO_BLOCKS * waves + SCALE_ROWS, spaxels), jnp.bfloat16)
    moment = jax.ShapeDtypeStruct((MOMENT_ROWS, spaxels), jnp.float32)
    moment_all = jax.ShapeDtypeStruct((devices, MOMENT_ROWS, spaxels), jnp.float32)
    params = pltpu.CompilerParams(vmem_limit_bytes=VMEM_LIMIT)
    circuit = circuit_of(tiles, lax.axis_size("wave"))
    reverse = [(j, i) for i, j in circuit]

    def swap(onward, back):
        axes = ("tile", "wave")
        return lax.ppermute(onward, axes, circuit), lax.ppermute(back, axes, reverse)

    chunks = CHUNKS if groups % CHUNKS == 0 else 1
    weights, held, onward, back = pl.pallas_call(
        rhs_kernel,
        out_shape=(jax.ShapeDtypeStruct(weights.shape, weights.dtype), window, rim, rim),
        in_specs=smem(4) + [pl.BlockSpec(memory_space=pltpu.HBM)] * 2,
        out_specs=tuple(vmem(4)),
        scratch_shapes=[
            pltpu.VMEM(fibre_data.shape, fibre_data.dtype),
            pltpu.VMEM(fibre_data.shape, jnp.float32),
            pltpu.SemaphoreType.DMA((chunks,)),
            pltpu.SemaphoreType.DMA,
        ],
        compiler_params=params,
        name="rhs",
    )(
        place,
        lane,
        live_count,
        index,
        pltpu.with_memory_space_constraint(fibre_data, pltpu.HBM),
        pltpu.with_memory_space_constraint(weights, pltpu.HBM),
    )
    scratch = [
        pltpu.VMEM((EXTENT, 2 * waves, spaxels), jnp.bfloat16),
        pltpu.VMEM((groups, 2 * waves, fibres), jnp.bfloat16),
    ]
    moments = jnp.zeros(moment.shape, jnp.float32)
    vectors = []
    for power in range(3):
        final = power == 2
        onward, back = swap(onward, back)
        out_rim = half_rim if final else rim
        vector, held, onward, back, moments = pl.pallas_call(
            functools.partial(step_kernel, tiles, power, final),
            out_shape=(window, window, out_rim, out_rim, moment_all if final else moment),
            in_specs=smem(4) + vmem(5),
            out_specs=tuple(vmem(5)),
            scratch_shapes=scratch,
            compiler_params=params,
            name=f"step{power}",
        )(place, lane, live_count, index, held, onward, back, moments, weights)
        vectors.append(vector)
    onward, back = swap(onward, back)
    moments = lax.all_to_all(moments, ("tile", "wave"), 0, 0)
    out = jax.ShapeDtypeStruct((waves, BLOCKS_DEV, spaxels), jnp.float32)
    answer, residual, steady = pl.pallas_call(
        functools.partial(final_kernel, tiles),
        out_shape=(out, out, jax.ShapeDtypeStruct((1,), jnp.int32)),
        in_specs=smem(2) + vmem(7),
        out_specs=tuple(vmem(2) + smem(1)),
        scratch_shapes=[pltpu.VMEM((BLOCKS_DEV, waves, spaxels), jnp.float32)],
        compiler_params=params,
        name="combine",
    )(place, lane, moments, *vectors, held, onward, back)

    def settled(held, onward, back):
        def decoded(code):
            scale = code[RIM * waves :].astype(jnp.float32) / CODE_PEAK
            code = code[: RIM * waves].astype(jnp.float32).reshape(-1, SCALE_ROWS, spaxels)
            root = jnp.sqrt(jnp.sqrt(jnp.sqrt(jnp.abs(code))))
            return (jnp.where(code < 0.0, -root, root) * scale).reshape(RIM, waves, spaxels)

        first = lane[0] == 0
        below = decoded(jnp.where(first, onward, back))
        above = decoded(jnp.where(first, back, onward))
        held = held.at[:RIM].add(jnp.where(place[0] > 0, below, 0.0))
        return held.at[EXTENT - RIM :].add(jnp.where(place[0] < tiles - 1, above, 0.0))

    def owned(vector):
        return vector[HALO_BLOCKS : HALO_BLOCKS + BLOCKS_DEV]

    def inner(first, second):
        return lax.psum(jnp.sum(owned(first) * owned(second)), ("tile", "wave"))

    def plain(operands):
        start, _, _ = operands
        none = jnp.zeros(rim.shape, rim.dtype)

        def iterate(_, state):
            total, left, direction, norm = state
            _, held, onward, back, _ = pl.pallas_call(
                functools.partial(step_kernel, tiles, 0, False),
                out_shape=(window, window, rim, rim, moment),
                in_specs=smem(4) + vmem(5),
                out_specs=tuple(vmem(5)),
                scratch_shapes=scratch,
                compiler_params=params,
                name="plain",
            )(
                place,
                lane,
                live_count,
                index,
                direction,
                none,
                none,
                jnp.zeros(moment.shape, jnp.float32),
                weights,
            )
            applied = settled(held, *swap(onward, back))
            size = norm / inner(direction, applied)
            total = total + size * direction
            left = left - size * applied
            following = inner(left, left)
            direction = left + (following / norm) * direction
            return total, left, direction, following

        state = (jnp.zeros_like(start), start, start, inner(start, start))
        total, left, _, _ = lax.fori_loop(0, ITERATIONS, iterate, state)
        return jnp.swapaxes(owned(total), 0, 1), jnp.swapaxes(owned(left), 0, 1)

    def kept(operands):
        return operands[1], operands[2]

    return lax.cond(steady[0] == 1, kept, plain, (vectors[0], answer, residual))


def solution(mesh):
    in_specs = (
        P("wave", "tile", None),
        P("wave", "tile", None, None, None),
        P("wave", "tile", None),
        P("tile"),
    )
    out_specs = (P("wave", "tile", None), P("wave", "tile", None))
    return jax.shard_map(shards, mesh=mesh, in_specs=in_specs, out_specs=out_specs, check_vma=False)
```

```python
import functools

import jax
import jax.numpy as jnp
from jax import lax
from jax.experimental import pallas as pl
from jax.experimental.pallas import tpu as pltpu
from jax.sharding import PartitionSpec as P

HALO_BLOCKS = 4
BLOCKS_DEV = 16
EXTENT = BLOCKS_DEV + 2 * HALO_BLOCKS
RIM = 2 * HALO_BLOCKS
TIKHONOV = 0.5
ITERATIONS = 3
SPREAD_LIMIT = 40.0
CHUNKS = 2
SCALE_ROWS = 16
CODE_PEAK = 32768.0
CODE_FLOOR = 1e-33
MOMENT_ROWS = 8
VMEM_LIMIT = 24 * 1024 * 1024


def split(value):
    upper = value.astype(jnp.bfloat16)
    lower = (value - upper.astype(jnp.float32)).astype(jnp.bfloat16)
    return upper, lower


def halves_sum(value):
    half = value.shape[0] // 2
    return value[:half] + value[half:]


def scatter(spread, place_ref, index_ref, group, partial_ref):
    lanes = partial_ref.shape[2]
    first = place_ref[0] * BLOCKS_DEV - HALO_BLOCKS
    for slot in range(index_ref.shape[0]):
        block = index_ref[slot, group] - first
        partial_ref[block] += spread[:, slot * lanes : (slot + 1) * lanes]


def spread_of(image, weights):
    return lax.dot_general(
        image, weights, (((1,), (1,)), ((), ())), preferred_element_type=jnp.float32
    )


def folded(value, rows, combine):
    parts = [value[start : start + rows] for start in range(0, value.shape[0], rows)]
    return functools.reduce(combine, parts)


def repeated(value, rows):
    return jnp.concatenate([value] * (rows // value.shape[0]), axis=0)


def encode(partial_ref, start, rim_ref):
    waves = partial_ref.shape[1]
    width = (rim_ref.shape[0] - SCALE_ROWS) // waves
    scales = rim_ref.at[width * waves :]
    peak = None
    for block in range(width):
        size = folded(jnp.abs(partial_ref[start + block]), 8, jnp.maximum)
        peak = size if peak is None else jnp.maximum(peak, size)
    scales[...] = repeated(jnp.maximum(peak, CODE_FLOOR), SCALE_ROWS).astype(jnp.bfloat16)
    gain = repeated(CODE_PEAK / scales[...].astype(jnp.float32), waves)
    for block in range(width):
        value = partial_ref[start + block] * gain
        for _ in range(3):
            value = value * jnp.abs(value)
        rim_ref[block * waves : (block + 1) * waves] = value.astype(jnp.bfloat16)


def decode_add(rim_ref, present, target_ref, start):
    waves = target_ref.shape[1]
    width = (rim_ref.shape[0] - SCALE_ROWS) // waves
    scale = rim_ref[width * waves :].astype(jnp.float32) / CODE_PEAK
    scale = repeated(jnp.where(present, scale, 0.0), waves)
    for block in range(width):
        code = rim_ref[block * waves : (block + 1) * waves].astype(jnp.float32)
        root = jnp.sqrt(jnp.sqrt(jnp.sqrt(jnp.abs(code))))
        target_ref[start + block] += jnp.where(code < 0.0, -root, root) * scale


def rim_top(extent, rim_ref, waves):
    return extent - (rim_ref.shape[0] - SCALE_ROWS) // waves


def rim_start(lane_ref, extent, rim_ref, waves, upper):
    return jnp.where(upper == (lane_ref[0] == 0), rim_top(extent, rim_ref, waves), 0)


def emit_rims(lane_ref, partial_ref, onward_ref, return_ref):
    extent, waves = partial_ref.shape[:2]
    for upper, rim_ref in ((True, onward_ref), (False, return_ref)):
        encode(partial_ref, rim_start(lane_ref, extent, rim_ref, waves, upper), rim_ref)


def add_rims(tiles, place_ref, lane_ref, target_ref, onward_in_ref, return_in_ref):
    extent, waves = target_ref.shape[:2]
    for upper, rim_ref in ((False, onward_in_ref), (True, return_in_ref)):
        start = rim_start(lane_ref, extent, rim_ref, waves, upper)
        end_tile = jnp.where(start > 0, tiles - 1, 0)
        decode_add(rim_ref, place_ref[0] != end_tile, target_ref, start)


def rhs_kernel(
    place_ref,
    lane_ref,
    live_ref,
    index_ref,
    data_ref,
    source_ref,
    kernels_ref,
    partial_ref,
    onward_ref,
    return_ref,
    narrow_ref,
    wide_ref,
    sems,
    data_sem,
):
    groups, slots, spaxels, fibres = kernels_ref.shape
    chunks = sems.shape[0]
    size = groups // chunks

    def copy(chunk):
        part = pl.ds(chunk * size, size)
        return pltpu.make_async_copy(source_ref.at[part], kernels_ref.at[part], sems.at[chunk])

    data_copy = pltpu.make_async_copy(data_ref, narrow_ref, data_sem)
    data_copy.start()
    for chunk in range(chunks):
        copy(chunk).start()
    partial_ref[...] = jnp.zeros_like(partial_ref)
    data_copy.wait()
    wide_ref[...] = narrow_ref[...].astype(jnp.float32)
    live = live_ref[0]
    for chunk in range(chunks):
        copy(chunk).wait()
        for group in range(chunk * size, (chunk + 1) * size):
            data = jnp.where(group < live, wide_ref[:, group, :], 0.0).astype(jnp.bfloat16)
            spread = spread_of(data, kernels_ref[group].reshape(slots * spaxels, fibres))
            scatter(spread, place_ref, index_ref, group, partial_ref)
    emit_rims(lane_ref, partial_ref, onward_ref, return_ref)


def step_kernel(
    tiles,
    power,
    final,
    place_ref,
    lane_ref,
    live_ref,
    index_ref,
    held_ref,
    onward_in_ref,
    return_in_ref,
    moments_in_ref,
    kernels_ref,
    vector_ref,
    partial_ref,
    onward_ref,
    return_ref,
    moments_ref,
    operand_ref,
    image_ref,
):
    groups, slots, spaxels, fibres = kernels_ref.shape
    waves = held_ref.shape[1]
    live = live_ref[0]
    first_block = place_ref[0] * BLOCKS_DEV - HALO_BLOCKS
    vector_ref[...] = held_ref[...]
    add_rims(tiles, place_ref, lane_ref, vector_ref, onward_in_ref, return_in_ref)
    square = jnp.zeros(vector_ref.shape[1:], jnp.float32)
    for block in range(EXTENT):
        value = vector_ref[block]
        operand_ref[block, :waves], operand_ref[block, waves:] = split(value)
        if HALO_BLOCKS <= block < HALO_BLOCKS + BLOCKS_DEV:
            square = square + value * value
    partial_ref[...] = jnp.zeros_like(partial_ref)
    energy = jnp.zeros((waves, fibres), jnp.float32)
    for group in range(groups):
        picked = jnp.concatenate(
            [operand_ref[index_ref[slot, group] - first_block] for slot in range(slots)], axis=1
        )
        weights = kernels_ref[group].reshape(slots * spaxels, fibres)
        image = halves_sum(jnp.dot(picked, weights, preferred_element_type=jnp.float32))
        image = jnp.where(group < live, image, 0.0)
        energy = energy + image * image
        image_ref[group, :waves], image_ref[group, waves:] = split(image)
    for group in range(groups):
        weights = kernels_ref[group].reshape(slots * spaxels, fibres)
        spread = halves_sum(spread_of(image_ref[group], weights))
        scatter(spread, place_ref, index_ref, group, partial_ref)
    emit_rims(lane_ref, partial_ref, onward_ref, return_ref)
    for block in range(EXTENT):
        partial_ref[block] += TIKHONOV * vector_ref[block]
    square_row = jnp.sum(square, axis=0, keepdims=True)
    energy_row = jnp.sum(energy, axis=0, keepdims=True) + TIKHONOV * square_row
    rows = lax.broadcasted_iota(jnp.int32, moments_in_ref.shape, 0)
    moments = jnp.where(
        rows == 2 * power,
        square_row,
        jnp.where(rows == 2 * power + 1, energy_row, moments_in_ref[...]),
    )
    moments_ref[...] = jnp.broadcast_to(moments, moments_ref.shape) if final else moments


def coefficients(moments, steps):
    def inner(first, second, shift):
        total = 0.0
        for i, a in enumerate(first):
            for j, b in enumerate(second):
                if a is not None and b is not None:
                    total = total + a * b * moments[i + j + shift]
        return total

    one = jnp.ones_like(moments[0])
    residual, direction = [one], [one]
    answer = []
    current = inner(residual, residual, 0)
    for step in range(steps):
        size = current / inner(direction, direction, 1)
        answer = [
            size * d + (answer[i] if i < len(answer) else 0.0) for i, d in enumerate(direction)
        ]
        shifted = [0.0] + [-size * d for d in direction]
        residual = [
            s + (residual[i] if i < len(residual) else 0.0) for i, s in enumerate(shifted)
        ]
        if step + 1 < steps:
            following = inner(residual, residual, 0)
            ratio = following / current
            direction = [
                r + (ratio * direction[i] if i < len(direction) else 0.0)
                for i, r in enumerate(residual)
            ]
            current = following
    return answer, residual


def final_kernel(
    tiles,
    place_ref,
    lane_ref,
    moments_ref,
    first_ref,
    second_ref,
    third_ref,
    held_ref,
    onward_in_ref,
    return_in_ref,
    solution_ref,
    residual_ref,
    flag_ref,
    last_ref,
    solution_buf,
    residual_buf,
    sems,
):
    sums = moments_ref[0]
    for source in range(1, moments_ref.shape[0]):
        sums = sums + moments_ref[source]
    sums = jnp.sum(sums, axis=1, keepdims=True)
    lanes = first_ref.shape[2]
    raw = [jnp.broadcast_to(sums[row : row + 1], (1, lanes)) for row in range(6)]
    unit = raw[0] / raw[1]
    scaled, factor = [], 1.0 / raw[0]
    for row in range(6):
        scaled.append(raw[row] * factor)
        factor = factor * unit
    answer, residual = coefficients(scaled, ITERATIONS)
    sizes = [jnp.sqrt(scaled[2 * row]) for row in range(3)]
    sizes.append(scaled[5] / sizes[2])
    terms = sum(jnp.abs(c) * size for c, size in zip(residual, sizes))
    flag_ref[0] = jnp.min(jnp.where(terms <= SPREAD_LIMIT, 1, 0))
    power = jnp.ones_like(unit)
    answer_scaled, residual_scaled = [], []
    for row in range(4):
        residual_scaled.append(residual[row] * power)
        power = power * unit
        if row < 3:
            answer_scaled.append(answer[row] * power)
    last_ref[...] = held_ref[pl.ds(HALO_BLOCKS, BLOCKS_DEV)]
    add_rims(tiles, place_ref, lane_ref, last_ref, onward_in_ref, return_in_ref)
    for block in range(BLOCKS_DEV):
        inside = HALO_BLOCKS + block
        solution_buf[:, block, :] = (
            answer_scaled[0] * first_ref[inside]
            + answer_scaled[1] * second_ref[inside]
            + answer_scaled[2] * third_ref[inside]
        )
    solution_copy = pltpu.make_async_copy(solution_buf, solution_ref, sems.at[0])
    solution_copy.start()
    for block in range(BLOCKS_DEV):
        inside = HALO_BLOCKS + block
        residual_buf[:, block, :] = (
            first_ref[inside]
            + residual_scaled[1] * second_ref[inside]
            + residual_scaled[2] * third_ref[inside]
            + residual_scaled[3] * last_ref[block]
        )
    residual_copy = pltpu.make_async_copy(residual_buf, residual_ref, sems.at[1])
    residual_copy.start()
    solution_copy.wait()
    residual_copy.wait()


def vmem(count):
    return [pl.BlockSpec(memory_space=pltpu.VMEM)] * count


def smem(count):
    return [pl.BlockSpec(memory_space=pltpu.SMEM)] * count


def circuit_of(tiles, waves):
    pairs = []
    for wave in range(0, waves, 2):
        path = [tile * waves + wave for tile in range(tiles)]
        if wave + 1 < waves:
            path += [tile * waves + wave + 1 for tile in reversed(range(tiles))]
        pairs += [(node, path[(step + 1) % len(path)]) for step, node in enumerate(path)]
    return pairs


def shards(fibre_data, kernels, block_index, live_count):
    tiles, devices = lax.axis_size("tile"), lax.axis_size("tile") * lax.axis_size("wave")
    _, groups, slots, spaxels, fibres = kernels.shape
    waves = fibre_data.shape[0]
    place = lax.axis_index("tile").reshape(1)
    lane = (lax.axis_index("wave") % 2).reshape(1)
    index = jnp.swapaxes(block_index, 1, 2).reshape(slots, groups)
    weights = kernels.reshape(groups, slots, spaxels, fibres)
    window = jax.ShapeDtypeStruct((EXTENT, waves, spaxels), jnp.float32)
    rim = jax.ShapeDtypeStruct((RIM * waves + SCALE_ROWS, spaxels), jnp.bfloat16)
    half_rim = jax.ShapeDtypeStruct((HALO_BLOCKS * waves + SCALE_ROWS, spaxels), jnp.bfloat16)
    moment = jax.ShapeDtypeStruct((MOMENT_ROWS, spaxels), jnp.float32)
    moment_all = jax.ShapeDtypeStruct((devices, MOMENT_ROWS, spaxels), jnp.float32)
    params = pltpu.CompilerParams(vmem_limit_bytes=VMEM_LIMIT)
    circuit = circuit_of(tiles, lax.axis_size("wave"))
    reverse = [(j, i) for i, j in circuit]

    def swap(onward, back):
        axes = ("tile", "wave")
        return lax.ppermute(onward, axes, circuit), lax.ppermute(back, axes, reverse)

    chunks = CHUNKS if groups % CHUNKS == 0 else 1
    weights, held, onward, back = pl.pallas_call(
        rhs_kernel,
        out_shape=(jax.ShapeDtypeStruct(weights.shape, weights.dtype), window, rim, rim),
        in_specs=smem(4) + [pl.BlockSpec(memory_space=pltpu.HBM)] * 2,
        out_specs=tuple(vmem(4)),
        scratch_shapes=[
            pltpu.VMEM(fibre_data.shape, fibre_data.dtype),
            pltpu.VMEM(fibre_data.shape, jnp.float32),
            pltpu.SemaphoreType.DMA((chunks,)),
            pltpu.SemaphoreType.DMA,
        ],
        compiler_params=params,
        name="rhs",
    )(
        place,
        lane,
        live_count,
        pltpu.with_memory_space_constraint(index, pltpu.HBM),
        pltpu.with_memory_space_constraint(fibre_data, pltpu.HBM),
        pltpu.with_memory_space_constraint(weights, pltpu.HBM),
    )
    scratch = [
        pltpu.VMEM((EXTENT, 2 * waves, spaxels), jnp.bfloat16),
        pltpu.VMEM((groups, 2 * waves, fibres), jnp.bfloat16),
    ]
    moments = jnp.zeros(moment.shape, jnp.float32)
    vectors = []
    for power in range(3):
        final = power == 2
        onward, back = swap(onward, back)
        out_rim = half_rim if final else rim
        vector, held, onward, back, moments = pl.pallas_call(
            functools.partial(step_kernel, tiles, power, final),
            out_shape=(window, window, out_rim, out_rim, moment_all if final else moment),
            in_specs=smem(4) + vmem(5),
            out_specs=tuple(vmem(5)),
            scratch_shapes=scratch,
            compiler_params=params,
            name=f"step{power}",
        )(place, lane, live_count, index, held, onward, back, moments, weights)
        vectors.append(vector)
    onward, back = swap(onward, back)
    moments = lax.all_to_all(moments, ("tile", "wave"), 0, 0)
    out = pltpu.HBM((waves, BLOCKS_DEV, spaxels), jnp.float32)
    answer, residual, steady = pl.pallas_call(
        functools.partial(final_kernel, tiles),
        out_shape=(out, out, jax.ShapeDtypeStruct((1,), jnp.int32)),
        in_specs=smem(2) + vmem(7),
        out_specs=tuple([pl.BlockSpec(memory_space=pltpu.HBM)] * 2 + smem(1)),
        scratch_shapes=[
            pltpu.VMEM((BLOCKS_DEV, waves, spaxels), jnp.float32),
            pltpu.VMEM((waves, BLOCKS_DEV, spaxels), jnp.float32),
            pltpu.VMEM((waves, BLOCKS_DEV, spaxels), jnp.float32),
            pltpu.SemaphoreType.DMA((2,)),
        ],
        compiler_params=params,
        name="combine",
    )(place, lane, moments, *vectors, held, onward, back)

    def settled(held, onward, back):
        def decoded(code):
            scale = code[RIM * waves :].astype(jnp.float32) / CODE_PEAK
            code = code[: RIM * waves].astype(jnp.float32).reshape(-1, SCALE_ROWS, spaxels)
            root = jnp.sqrt(jnp.sqrt(jnp.sqrt(jnp.abs(code))))
            return (jnp.where(code < 0.0, -root, root) * scale).reshape(RIM, waves, spaxels)

        first = lane[0] == 0
        below = decoded(jnp.where(first, onward, back))
        above = decoded(jnp.where(first, back, onward))
        held = held.at[:RIM].add(jnp.where(place[0] > 0, below, 0.0))
        return held.at[EXTENT - RIM :].add(jnp.where(place[0] < tiles - 1, above, 0.0))

    def owned(vector):
        return vector[HALO_BLOCKS : HALO_BLOCKS + BLOCKS_DEV]

    def inner(first, second):
        return lax.psum(jnp.sum(owned(first) * owned(second)), ("tile", "wave"))

    def plain(operands):
        start, _, _ = operands
        none = jnp.zeros(rim.shape, rim.dtype)

        def iterate(_, state):
            total, left, direction, norm = state
            _, held, onward, back, _ = pl.pallas_call(
                functools.partial(step_kernel, tiles, 0, False),
                out_shape=(window, window, rim, rim, moment),
                in_specs=smem(4) + vmem(5),
                out_specs=tuple(vmem(5)),
                scratch_shapes=scratch,
                compiler_params=params,
                name="plain",
            )(
                place,
                lane,
                live_count,
                index,
                direction,
                none,
                none,
                jnp.zeros(moment.shape, jnp.float32),
                weights,
            )
            applied = settled(held, *swap(onward, back))
            size = norm / inner(direction, applied)
            total = total + size * direction
            left = left - size * applied
            following = inner(left, left)
            direction = left + (following / norm) * direction
            return total, left, direction, following

        state = (jnp.zeros_like(start), start, start, inner(start, start))
        total, left, _, _ = lax.fori_loop(0, ITERATIONS, iterate, state)
        return jnp.swapaxes(owned(total), 0, 1), jnp.swapaxes(owned(left), 0, 1)

    def kept(operands):
        return operands[1], operands[2]

    return lax.cond(steady[0] == 1, kept, plain, (vectors[0], answer, residual))


def solution(mesh):
    in_specs = (
        P("wave", "tile", None),
        P("wave", "tile", None, None, None),
        P("wave", "tile", None),
        P("tile"),
    )
    out_specs = (P("wave", "tile", None), P("wave", "tile", None))
    return jax.shard_map(shards, mesh=mesh, in_specs=in_specs, out_specs=out_specs, check_vma=False)
```

```python
import functools

import jax
import jax.numpy as jnp
from jax import lax
from jax.experimental import pallas as pl
from jax.experimental.pallas import tpu as pltpu
from jax.sharding import PartitionSpec as P

HALO_BLOCKS = 4
BLOCKS_DEV = 16
EXTENT = BLOCKS_DEV + 2 * HALO_BLOCKS
RIM = 2 * HALO_BLOCKS
TIKHONOV = 0.5
ITERATIONS = 3
SPREAD_LIMIT = 40.0
CHUNKS = 2
SCALE_ROWS = 16
CODE_PEAK = 32768.0
CODE_FLOOR = 1e-33
MOMENT_ROWS = 8
VMEM_LIMIT = 24 * 1024 * 1024


def split(value):
    upper = value.astype(jnp.bfloat16)
    lower = (value - upper.astype(jnp.float32)).astype(jnp.bfloat16)
    return upper, lower


def halves_sum(value):
    half = value.shape[0] // 2
    return value[:half] + value[half:]


def scatter(spread, place_ref, index_ref, group, partial_ref):
    lanes = partial_ref.shape[2]
    first = place_ref[0] * BLOCKS_DEV - HALO_BLOCKS
    for slot in range(index_ref.shape[0]):
        block = index_ref[slot, group] - first
        partial_ref[block] += spread[:, slot * lanes : (slot + 1) * lanes]


def folded(value, rows, combine):
    parts = [value[start : start + rows] for start in range(0, value.shape[0], rows)]
    return functools.reduce(combine, parts)


def repeated(value, rows):
    return jnp.concatenate([value] * (rows // value.shape[0]), axis=0)


def encode(partial_ref, start, rim_ref):
    waves = partial_ref.shape[1]
    width = (rim_ref.shape[0] - SCALE_ROWS) // waves
    scales = rim_ref.at[width * waves :]
    peak = None
    for block in range(width):
        size = folded(jnp.abs(partial_ref[start + block]), 8, jnp.maximum)
        peak = size if peak is None else jnp.maximum(peak, size)
    scales[...] = repeated(jnp.maximum(peak, CODE_FLOOR), SCALE_ROWS).astype(jnp.bfloat16)
    gain = repeated(CODE_PEAK / scales[...].astype(jnp.float32), waves)
    for block in range(width):
        value = partial_ref[start + block] * gain
        for _ in range(3):
            value = value * jnp.abs(value)
        rim_ref[block * waves : (block + 1) * waves] = value.astype(jnp.bfloat16)


def decode_add(rim_ref, present, target_ref, start):
    waves = target_ref.shape[1]
    width = (rim_ref.shape[0] - SCALE_ROWS) // waves
    scale = rim_ref[width * waves :].astype(jnp.float32) / CODE_PEAK
    scale = repeated(jnp.where(present, scale, 0.0), waves)
    for block in range(width):
        code = rim_ref[block * waves : (block + 1) * waves].astype(jnp.float32)
        root = jnp.sqrt(jnp.sqrt(jnp.sqrt(jnp.abs(code))))
        target_ref[start + block] += jnp.where(code < 0.0, -root, root) * scale


def rim_top(extent, rim_ref, waves):
    return extent - (rim_ref.shape[0] - SCALE_ROWS) // waves


def rim_start(lane_ref, extent, rim_ref, waves, upper):
    return jnp.where(upper == (lane_ref[0] == 0), rim_top(extent, rim_ref, waves), 0)


def emit_rims(lane_ref, partial_ref, onward_ref, return_ref):
    extent, waves = partial_ref.shape[:2]
    for upper, rim_ref in ((True, onward_ref), (False, return_ref)):
        encode(partial_ref, rim_start(lane_ref, extent, rim_ref, waves, upper), rim_ref)


def add_rims(tiles, place_ref, lane_ref, target_ref, onward_in_ref, return_in_ref):
    extent, waves = target_ref.shape[:2]
    for upper, rim_ref in ((False, onward_in_ref), (True, return_in_ref)):
        start = rim_start(lane_ref, extent, rim_ref, waves, upper)
        end_tile = jnp.where(start > 0, tiles - 1, 0)
        decode_add(rim_ref, place_ref[0] != end_tile, target_ref, start)


def rhs_kernel(
    place_ref,
    lane_ref,
    live_ref,
    index_ref,
    data_ref,
    source_ref,
    kernels_ref,
    turned_ref,
    partial_ref,
    onward_ref,
    return_ref,
    narrow_ref,
    wide_ref,
    sems,
    data_sem,
):
    groups, slots, spaxels, fibres = kernels_ref.shape
    chunks = sems.shape[0]
    size = groups // chunks

    def copy(chunk):
        part = pl.ds(chunk * size, size)
        return pltpu.make_async_copy(source_ref.at[part], kernels_ref.at[part], sems.at[chunk])

    data_copy = pltpu.make_async_copy(data_ref, narrow_ref, data_sem)
    data_copy.start()
    for chunk in range(chunks):
        copy(chunk).start()
    partial_ref[...] = jnp.zeros_like(partial_ref)
    data_copy.wait()
    wide_ref[...] = narrow_ref[...].astype(jnp.float32)
    live = live_ref[0]
    for chunk in range(chunks):
        copy(chunk).wait()
        for group in range(chunk * size, (chunk + 1) * size):
            data = jnp.where(group < live, wide_ref[:, group, :], 0.0).astype(jnp.bfloat16)
            turned_ref[group] = kernels_ref[group].reshape(slots * spaxels, fibres).T
            spread = jnp.dot(data, turned_ref[group], preferred_element_type=jnp.float32)
            scatter(spread, place_ref, index_ref, group, partial_ref)
    emit_rims(lane_ref, partial_ref, onward_ref, return_ref)


def step_kernel(
    tiles,
    power,
    final,
    place_ref,
    lane_ref,
    live_ref,
    index_ref,
    held_ref,
    onward_in_ref,
    return_in_ref,
    moments_in_ref,
    kernels_ref,
    turned_ref,
    vector_ref,
    partial_ref,
    onward_ref,
    return_ref,
    moments_ref,
    operand_ref,
    image_ref,
):
    groups, slots, spaxels, fibres = kernels_ref.shape
    waves = held_ref.shape[1]
    live = live_ref[0]
    first_block = place_ref[0] * BLOCKS_DEV - HALO_BLOCKS
    vector_ref[...] = held_ref[...]
    add_rims(tiles, place_ref, lane_ref, vector_ref, onward_in_ref, return_in_ref)
    square = jnp.zeros(vector_ref.shape[1:], jnp.float32)
    for block in range(EXTENT):
        value = vector_ref[block]
        operand_ref[block, :waves], operand_ref[block, waves:] = split(value)
        if HALO_BLOCKS <= block < HALO_BLOCKS + BLOCKS_DEV:
            square = square + value * value
    partial_ref[...] = jnp.zeros_like(partial_ref)
    energy = jnp.zeros((waves, fibres), jnp.float32)
    for group in range(groups):
        picked = jnp.concatenate(
            [operand_ref[index_ref[slot, group] - first_block] for slot in range(slots)], axis=1
        )
        weights = kernels_ref[group].reshape(slots * spaxels, fibres)
        image = halves_sum(jnp.dot(picked, weights, preferred_element_type=jnp.float32))
        image = jnp.where(group < live, image, 0.0)
        energy = energy + image * image
        image_ref[group, :waves], image_ref[group, waves:] = split(image)
    for group in range(groups):
        spread = halves_sum(
            jnp.dot(image_ref[group], turned_ref[group], preferred_element_type=jnp.float32)
        )
        scatter(spread, place_ref, index_ref, group, partial_ref)
    emit_rims(lane_ref, partial_ref, onward_ref, return_ref)
    for block in range(EXTENT):
        partial_ref[block] += TIKHONOV * vector_ref[block]
    square_row = jnp.sum(square, axis=0, keepdims=True)
    energy_row = jnp.sum(energy, axis=0, keepdims=True) + TIKHONOV * square_row
    rows = lax.broadcasted_iota(jnp.int32, moments_in_ref.shape, 0)
    moments = jnp.where(
        rows == 2 * power,
        square_row,
        jnp.where(rows == 2 * power + 1, energy_row, moments_in_ref[...]),
    )
    moments_ref[...] = jnp.broadcast_to(moments, moments_ref.shape) if final else moments


def coefficients(moments, steps):
    def inner(first, second, shift):
        total = 0.0
        for i, a in enumerate(first):
            for j, b in enumerate(second):
                if a is not None and b is not None:
                    total = total + a * b * moments[i + j + shift]
        return total

    one = jnp.ones_like(moments[0])
    residual, direction = [one], [one]
    answer = []
    current = inner(residual, residual, 0)
    for step in range(steps):
        size = current / inner(direction, direction, 1)
        answer = [
            size * d + (answer[i] if i < len(answer) else 0.0) for i, d in enumerate(direction)
        ]
        shifted = [0.0] + [-size * d for d in direction]
        residual = [
            s + (residual[i] if i < len(residual) else 0.0) for i, s in enumerate(shifted)
        ]
        if step + 1 < steps:
            following = inner(residual, residual, 0)
            ratio = following / current
            direction = [
                r + (ratio * direction[i] if i < len(direction) else 0.0)
                for i, r in enumerate(residual)
            ]
            current = following
    return answer, residual


def final_kernel(
    tiles,
    place_ref,
    lane_ref,
    moments_ref,
    first_ref,
    second_ref,
    third_ref,
    held_ref,
    onward_in_ref,
    return_in_ref,
    solution_ref,
    residual_ref,
    flag_ref,
    last_ref,
    solution_buf,
    residual_buf,
    sems,
):
    sums = moments_ref[0]
    for source in range(1, moments_ref.shape[0]):
        sums = sums + moments_ref[source]
    sums = jnp.sum(sums, axis=1, keepdims=True)
    lanes = first_ref.shape[2]
    raw = [jnp.broadcast_to(sums[row : row + 1], (1, lanes)) for row in range(6)]
    unit = raw[0] / raw[1]
    scaled, factor = [], 1.0 / raw[0]
    for row in range(6):
        scaled.append(raw[row] * factor)
        factor = factor * unit
    answer, residual = coefficients(scaled, ITERATIONS)
    sizes = [jnp.sqrt(scaled[2 * row]) for row in range(3)]
    sizes.append(scaled[5] / sizes[2])
    terms = sum(jnp.abs(c) * size for c, size in zip(residual, sizes))
    flag_ref[0] = jnp.min(jnp.where(terms <= SPREAD_LIMIT, 1, 0))
    power = jnp.ones_like(unit)
    answer_scaled, residual_scaled = [], []
    for row in range(4):
        residual_scaled.append(residual[row] * power)
        power = power * unit
        if row < 3:
            answer_scaled.append(answer[row] * power)
    last_ref[...] = held_ref[pl.ds(HALO_BLOCKS, BLOCKS_DEV)]
    add_rims(tiles, place_ref, lane_ref, last_ref, onward_in_ref, return_in_ref)
    for block in range(BLOCKS_DEV):
        inside = HALO_BLOCKS + block
        solution_buf[:, block, :] = (
            answer_scaled[0] * first_ref[inside]
            + answer_scaled[1] * second_ref[inside]
            + answer_scaled[2] * third_ref[inside]
        )
    solution_copy = pltpu.make_async_copy(solution_buf, solution_ref, sems.at[0])
    solution_copy.start()
    for block in range(BLOCKS_DEV):
        inside = HALO_BLOCKS + block
        residual_buf[:, block, :] = (
            first_ref[inside]
            + residual_scaled[1] * second_ref[inside]
            + residual_scaled[2] * third_ref[inside]
            + residual_scaled[3] * last_ref[block]
        )
    residual_copy = pltpu.make_async_copy(residual_buf, residual_ref, sems.at[1])
    residual_copy.start()
    solution_copy.wait()
    residual_copy.wait()


def vmem(count):
    return [pl.BlockSpec(memory_space=pltpu.VMEM)] * count


def smem(count):
    return [pl.BlockSpec(memory_space=pltpu.SMEM)] * count


def circuit_of(tiles, waves):
    pairs = []
    for wave in range(0, waves, 2):
        path = [tile * waves + wave for tile in range(tiles)]
        if wave + 1 < waves:
            path += [tile * waves + wave + 1 for tile in reversed(range(tiles))]
        pairs += [(node, path[(step + 1) % len(path)]) for step, node in enumerate(path)]
    return pairs


def shards(fibre_data, kernels, block_index, live_count):
    tiles, devices = lax.axis_size("tile"), lax.axis_size("tile") * lax.axis_size("wave")
    _, groups, slots, spaxels, fibres = kernels.shape
    waves = fibre_data.shape[0]
    place = lax.axis_index("tile").reshape(1)
    lane = (lax.axis_index("wave") % 2).reshape(1)
    index = jnp.swapaxes(block_index, 1, 2).reshape(slots, groups)
    source = kernels.reshape(groups, slots, spaxels, fibres)
    turned = jax.ShapeDtypeStruct((groups, fibres, slots * spaxels), kernels.dtype)
    window = jax.ShapeDtypeStruct((EXTENT, waves, spaxels), jnp.float32)
    rim = jax.ShapeDtypeStruct((RIM * waves + SCALE_ROWS, spaxels), jnp.bfloat16)
    half_rim = jax.ShapeDtypeStruct((HALO_BLOCKS * waves + SCALE_ROWS, spaxels), jnp.bfloat16)
    moment = jax.ShapeDtypeStruct((MOMENT_ROWS, spaxels), jnp.float32)
    moment_all = jax.ShapeDtypeStruct((devices, MOMENT_ROWS, spaxels), jnp.float32)
    params = pltpu.CompilerParams(vmem_limit_bytes=VMEM_LIMIT)
    circuit = circuit_of(tiles, lax.axis_size("wave"))
    reverse = [(j, i) for i, j in circuit]

    def swap(onward, back):
        axes = ("tile", "wave")
        return lax.ppermute(onward, axes, circuit), lax.ppermute(back, axes, reverse)

    chunks = CHUNKS if groups % CHUNKS == 0 else 1
    weights, turned, held, onward, back = pl.pallas_call(
        rhs_kernel,
        out_shape=(jax.ShapeDtypeStruct(source.shape, source.dtype), turned, window, rim, rim),
        in_specs=smem(4) + [pl.BlockSpec(memory_space=pltpu.HBM)] * 2,
        out_specs=tuple(vmem(5)),
        scratch_shapes=[
            pltpu.VMEM(fibre_data.shape, fibre_data.dtype),
            pltpu.VMEM(fibre_data.shape, jnp.float32),
            pltpu.SemaphoreType.DMA((chunks,)),
            pltpu.SemaphoreType.DMA,
        ],
        compiler_params=params,
        name="rhs",
    )(
        place,
        lane,
        live_count,
        pltpu.with_memory_space_constraint(index, pltpu.HBM),
        pltpu.with_memory_space_constraint(fibre_data, pltpu.HBM),
        pltpu.with_memory_space_constraint(source, pltpu.HBM),
    )
    scratch = [
        pltpu.VMEM((EXTENT, 2 * waves, spaxels), jnp.bfloat16),
        pltpu.VMEM((groups, 2 * waves, fibres), jnp.bfloat16),
    ]
    moments = jnp.zeros(moment.shape, jnp.float32)
    vectors = []
    for power in range(3):
        final = power == 2
        onward, back = swap(onward, back)
        out_rim = half_rim if final else rim
        vector, held, onward, back, moments = pl.pallas_call(
            functools.partial(step_kernel, tiles, power, final),
            out_shape=(window, window, out_rim, out_rim, moment_all if final else moment),
            in_specs=smem(4) + vmem(6),
            out_specs=tuple(vmem(5)),
            scratch_shapes=scratch,
            compiler_params=params,
            name=f"step{power}",
        )(place, lane, live_count, index, held, onward, back, moments, weights, turned)
        vectors.append(vector)
    onward, back = swap(onward, back)
    moments = lax.all_to_all(moments, ("tile", "wave"), 0, 0)
    out = pltpu.HBM((waves, BLOCKS_DEV, spaxels), jnp.float32)
    answer, residual, steady = pl.pallas_call(
        functools.partial(final_kernel, tiles),
        out_shape=(out, out, jax.ShapeDtypeStruct((1,), jnp.int32)),
        in_specs=smem(2) + vmem(7),
        out_specs=tuple([pl.BlockSpec(memory_space=pltpu.HBM)] * 2 + smem(1)),
        scratch_shapes=[
            pltpu.VMEM((BLOCKS_DEV, waves, spaxels), jnp.float32),
            pltpu.VMEM((waves, BLOCKS_DEV, spaxels), jnp.float32),
            pltpu.VMEM((waves, BLOCKS_DEV, spaxels), jnp.float32),
            pltpu.SemaphoreType.DMA((2,)),
        ],
        compiler_params=params,
        name="combine",
    )(place, lane, moments, *vectors, held, onward, back)

    def settled(held, onward, back):
        def decoded(code):
            scale = code[RIM * waves :].astype(jnp.float32) / CODE_PEAK
            code = code[: RIM * waves].astype(jnp.float32).reshape(-1, SCALE_ROWS, spaxels)
            root = jnp.sqrt(jnp.sqrt(jnp.sqrt(jnp.abs(code))))
            return (jnp.where(code < 0.0, -root, root) * scale).reshape(RIM, waves, spaxels)

        first = lane[0] == 0
        below = decoded(jnp.where(first, onward, back))
        above = decoded(jnp.where(first, back, onward))
        held = held.at[:RIM].add(jnp.where(place[0] > 0, below, 0.0))
        return held.at[EXTENT - RIM :].add(jnp.where(place[0] < tiles - 1, above, 0.0))

    def owned(vector):
        return vector[HALO_BLOCKS : HALO_BLOCKS + BLOCKS_DEV]

    def inner(first, second):
        return lax.psum(jnp.sum(owned(first) * owned(second)), ("tile", "wave"))

    def plain(operands):
        start, _, _ = operands
        none = jnp.zeros(rim.shape, rim.dtype)

        def iterate(_, state):
            total, left, direction, norm = state
            _, held, onward, back, _ = pl.pallas_call(
                functools.partial(step_kernel, tiles, 0, False),
                out_shape=(window, window, rim, rim, moment),
                in_specs=smem(4) + vmem(6),
                out_specs=tuple(vmem(5)),
                scratch_shapes=scratch,
                compiler_params=params,
                name="plain",
            )(
                place,
                lane,
                live_count,
                index,
                direction,
                none,
                none,
                jnp.zeros(moment.shape, jnp.float32),
                source,
                jnp.swapaxes(source.reshape(groups, slots * spaxels, fibres), 1, 2),
            )
            applied = settled(held, *swap(onward, back))
            size = norm / inner(direction, applied)
            total = total + size * direction
            left = left - size * applied
            following = inner(left, left)
            direction = left + (following / norm) * direction
            return total, left, direction, following

        state = (jnp.zeros_like(start), start, start, inner(start, start))
        total, left, _, _ = lax.fori_loop(0, ITERATIONS, iterate, state)
        return jnp.swapaxes(owned(total), 0, 1), jnp.swapaxes(owned(left), 0, 1)

    def kept(operands):
        return operands[1], operands[2]

    return lax.cond(steady[0] == 1, kept, plain, (vectors[0], answer, residual))


def solution(mesh):
    in_specs = (
        P("wave", "tile", None),
        P("wave", "tile", None, None, None),
        P("wave", "tile", None),
        P("tile"),
    )
    out_specs = (P("wave", "tile", None), P("wave", "tile", None))
    return jax.shard_map(shards, mesh=mesh, in_specs=in_specs, out_specs=out_specs, check_vma=False)
```

```python
import functools

import jax
import jax.numpy as jnp
from jax import lax
from jax.experimental import pallas as pl
from jax.experimental.pallas import tpu as pltpu
from jax.sharding import PartitionSpec as P

HALO_BLOCKS = 4
BLOCKS_DEV = 16
EXTENT = BLOCKS_DEV + 2 * HALO_BLOCKS
RIM = 2 * HALO_BLOCKS
TIKHONOV = 0.5
ITERATIONS = 3
SPREAD_LIMIT = 40.0
CHUNKS = 2
SCALE_ROWS = 16
CODE_PEAK = 32768.0
CODE_FLOOR = 1e-33
MOMENT_ROWS = 8
VMEM_LIMIT = 24 * 1024 * 1024


def split(value):
    upper = value.astype(jnp.bfloat16)
    lower = (value - upper.astype(jnp.float32)).astype(jnp.bfloat16)
    return upper, lower


def halves_sum(value):
    half = value.shape[0] // 2
    return value[:half] + value[half:]


def scatter(spread, place_ref, index_ref, group, partial_ref):
    lanes = partial_ref.shape[2]
    first = place_ref[0] * BLOCKS_DEV - HALO_BLOCKS
    for slot in range(index_ref.shape[0]):
        block = index_ref[slot, group] - first
        partial_ref[block] += spread[:, slot * lanes : (slot + 1) * lanes]


def folded(value, rows, combine):
    parts = [value[start : start + rows] for start in range(0, value.shape[0], rows)]
    return functools.reduce(combine, parts)


def repeated(value, rows):
    return jnp.concatenate([value] * (rows // value.shape[0]), axis=0)


def encode(partial_ref, start, rim_ref):
    waves = partial_ref.shape[1]
    width = (rim_ref.shape[0] - SCALE_ROWS) // waves
    scales = rim_ref.at[width * waves :]
    peak = None
    for block in range(width):
        size = folded(jnp.abs(partial_ref[start + block]), 8, jnp.maximum)
        peak = size if peak is None else jnp.maximum(peak, size)
    scales[...] = repeated(jnp.maximum(peak, CODE_FLOOR), SCALE_ROWS).astype(jnp.bfloat16)
    gain = repeated(CODE_PEAK / scales[...].astype(jnp.float32), waves)
    for block in range(width):
        value = partial_ref[start + block] * gain
        for _ in range(3):
            value = value * jnp.abs(value)
        rim_ref[block * waves : (block + 1) * waves] = value.astype(jnp.bfloat16)


def decode_add(rim_ref, present, target_ref, start):
    waves = target_ref.shape[1]
    width = (rim_ref.shape[0] - SCALE_ROWS) // waves
    scale = rim_ref[width * waves :].astype(jnp.float32) / CODE_PEAK
    scale = repeated(jnp.where(present, scale, 0.0), waves)
    for block in range(width):
        code = rim_ref[block * waves : (block + 1) * waves].astype(jnp.float32)
        root = jnp.sqrt(jnp.sqrt(jnp.sqrt(jnp.abs(code))))
        target_ref[start + block] += jnp.where(code < 0.0, -root, root) * scale


def rim_top(extent, rim_ref, waves):
    return extent - (rim_ref.shape[0] - SCALE_ROWS) // waves


def rim_start(lane_ref, extent, rim_ref, waves, upper):
    return jnp.where(upper == (lane_ref[0] == 0), rim_top(extent, rim_ref, waves), 0)


def emit_rims(lane_ref, partial_ref, onward_ref, return_ref):
    extent, waves = partial_ref.shape[:2]
    for upper, rim_ref in ((True, onward_ref), (False, return_ref)):
        encode(partial_ref, rim_start(lane_ref, extent, rim_ref, waves, upper), rim_ref)


def add_rims(tiles, place_ref, lane_ref, target_ref, onward_in_ref, return_in_ref):
    extent, waves = target_ref.shape[:2]
    for upper, rim_ref in ((False, onward_in_ref), (True, return_in_ref)):
        start = rim_start(lane_ref, extent, rim_ref, waves, upper)
        end_tile = jnp.where(start > 0, tiles - 1, 0)
        decode_add(rim_ref, place_ref[0] != end_tile, target_ref, start)


def rhs_kernel(
    place_ref,
    lane_ref,
    live_ref,
    index_ref,
    data_ref,
    source_ref,
    kernels_ref,
    turned_ref,
    partial_ref,
    onward_ref,
    return_ref,
    narrow_ref,
    wide_ref,
    sems,
    data_sem,
):
    groups, slots, spaxels, fibres = kernels_ref.shape
    chunks = sems.shape[0]
    size = groups // chunks

    def copy(chunk):
        part = pl.ds(chunk * size, size)
        return pltpu.make_async_copy(source_ref.at[part], kernels_ref.at[part], sems.at[chunk])

    data_copy = pltpu.make_async_copy(data_ref, narrow_ref, data_sem)
    data_copy.start()
    for chunk in range(chunks):
        copy(chunk).start()
    partial_ref[...] = jnp.zeros_like(partial_ref)
    data_copy.wait()
    wide_ref[...] = narrow_ref[...].astype(jnp.float32)
    live = live_ref[0]
    for chunk in range(chunks):
        copy(chunk).wait()
        for group in range(chunk * size, (chunk + 1) * size):
            data = jnp.where(group < live, wide_ref[:, group, :], 0.0).astype(jnp.bfloat16)
            turned_ref[group] = kernels_ref[group].reshape(slots * spaxels, fibres).T
            spread = jnp.dot(data, turned_ref[group], preferred_element_type=jnp.float32)
            scatter(spread, place_ref, index_ref, group, partial_ref)
    emit_rims(lane_ref, partial_ref, onward_ref, return_ref)


def step_kernel(
    tiles,
    power,
    final,
    place_ref,
    lane_ref,
    live_ref,
    index_ref,
    held_ref,
    onward_in_ref,
    return_in_ref,
    moments_in_ref,
    kernels_ref,
    turned_ref,
    vector_ref,
    partial_ref,
    onward_ref,
    return_ref,
    moments_ref,
    operand_ref,
    image_ref,
):
    groups, slots, spaxels, fibres = kernels_ref.shape
    waves = held_ref.shape[1]
    live = live_ref[0]
    first_block = place_ref[0] * BLOCKS_DEV - HALO_BLOCKS
    vector_ref[...] = held_ref[...]
    add_rims(tiles, place_ref, lane_ref, vector_ref, onward_in_ref, return_in_ref)
    square = jnp.zeros(vector_ref.shape[1:], jnp.float32)
    for block in range(EXTENT):
        value = vector_ref[block]
        operand_ref[block, :waves], operand_ref[block, waves:] = split(value)
        if HALO_BLOCKS <= block < HALO_BLOCKS + BLOCKS_DEV:
            square = square + value * value
    partial_ref[...] = jnp.zeros_like(partial_ref)
    energy = jnp.zeros((waves, fibres), jnp.float32)
    for group in range(groups):
        picked = jnp.concatenate(
            [operand_ref[index_ref[slot, group] - first_block] for slot in range(slots)], axis=1
        )
        weights = kernels_ref[group].reshape(slots * spaxels, fibres)
        image = halves_sum(jnp.dot(picked, weights, preferred_element_type=jnp.float32))
        image = jnp.where(group < live, image, 0.0)
        energy = energy + image * image
        image_ref[group, :waves], image_ref[group, waves:] = split(image)
    for group in range(groups):
        spread = halves_sum(
            jnp.dot(image_ref[group], turned_ref[group], preferred_element_type=jnp.float32)
        )
        scatter(spread, place_ref, index_ref, group, partial_ref)
    emit_rims(lane_ref, partial_ref, onward_ref, return_ref)
    for block in range(EXTENT):
        partial_ref[block] += TIKHONOV * vector_ref[block]
    square_row = jnp.sum(square, axis=0, keepdims=True)
    energy_row = jnp.sum(energy, axis=0, keepdims=True) + TIKHONOV * square_row
    rows = lax.broadcasted_iota(jnp.int32, moments_in_ref.shape, 0)
    moments = jnp.where(
        rows == 2 * power,
        square_row,
        jnp.where(rows == 2 * power + 1, energy_row, moments_in_ref[...]),
    )
    if not final:
        moments_ref[...] = moments
        return
    lanes = lax.broadcasted_iota(jnp.int32, moments.shape, 1)
    totals = jnp.sum(moments, axis=1, keepdims=True)
    packed = jnp.sum(jnp.where(lanes == rows, totals, 0.0), axis=0, keepdims=True)
    moments_ref[...] = jnp.broadcast_to(packed[None], moments_ref.shape)


def coefficients(moments, steps):
    def inner(first, second, shift):
        total = 0.0
        for i, a in enumerate(first):
            for j, b in enumerate(second):
                if a is not None and b is not None:
                    total = total + a * b * moments[i + j + shift]
        return total

    one = jnp.ones_like(moments[0])
    residual, direction = [one], [one]
    answer = []
    current = inner(residual, residual, 0)
    for step in range(steps):
        size = current / inner(direction, direction, 1)
        answer = [
            size * d + (answer[i] if i < len(answer) else 0.0) for i, d in enumerate(direction)
        ]
        shifted = [0.0] + [-size * d for d in direction]
        residual = [
            s + (residual[i] if i < len(residual) else 0.0) for i, s in enumerate(shifted)
        ]
        if step + 1 < steps:
            following = inner(residual, residual, 0)
            ratio = following / current
            direction = [
                r + (ratio * direction[i] if i < len(direction) else 0.0)
                for i, r in enumerate(residual)
            ]
            current = following
    return answer, residual


def final_kernel(
    tiles,
    place_ref,
    lane_ref,
    moments_ref,
    first_ref,
    second_ref,
    third_ref,
    held_ref,
    onward_in_ref,
    return_in_ref,
    solution_ref,
    residual_ref,
    flag_ref,
    last_ref,
    solution_buf,
    residual_buf,
    sems,
):
    sums = jnp.sum(moments_ref[:, 0, :], axis=0, keepdims=True)
    lanes = lax.broadcasted_iota(jnp.int32, sums.shape, 1)
    raw = [
        jnp.broadcast_to(
            jnp.sum(jnp.where(lanes == row, sums, 0.0), axis=1, keepdims=True), sums.shape
        )
        for row in range(6)
    ]
    unit = raw[0] / raw[1]
    scaled, factor = [], 1.0 / raw[0]
    for row in range(6):
        scaled.append(raw[row] * factor)
        factor = factor * unit
    answer, residual = coefficients(scaled, ITERATIONS)
    sizes = [jnp.sqrt(scaled[2 * row]) for row in range(3)]
    sizes.append(scaled[5] / sizes[2])
    terms = sum(jnp.abs(c) * size for c, size in zip(residual, sizes))
    flag_ref[0] = jnp.min(jnp.where(terms <= SPREAD_LIMIT, 1, 0))
    power = jnp.ones_like(unit)
    answer_scaled, residual_scaled = [], []
    for row in range(4):
        residual_scaled.append(residual[row] * power)
        power = power * unit
        if row < 3:
            answer_scaled.append(answer[row] * power)
    last_ref[...] = held_ref[pl.ds(HALO_BLOCKS, BLOCKS_DEV)]
    add_rims(tiles, place_ref, lane_ref, last_ref, onward_in_ref, return_in_ref)
    for block in range(BLOCKS_DEV):
        inside = HALO_BLOCKS + block
        solution_buf[:, block, :] = (
            answer_scaled[0] * first_ref[inside]
            + answer_scaled[1] * second_ref[inside]
            + answer_scaled[2] * third_ref[inside]
        )
    solution_copy = pltpu.make_async_copy(solution_buf, solution_ref, sems.at[0])
    solution_copy.start()
    for block in range(BLOCKS_DEV):
        inside = HALO_BLOCKS + block
        residual_buf[:, block, :] = (
            first_ref[inside]
            + residual_scaled[1] * second_ref[inside]
            + residual_scaled[2] * third_ref[inside]
            + residual_scaled[3] * last_ref[block]
        )
    residual_copy = pltpu.make_async_copy(residual_buf, residual_ref, sems.at[1])
    residual_copy.start()
    solution_copy.wait()
    residual_copy.wait()


def vmem(count):
    return [pl.BlockSpec(memory_space=pltpu.VMEM)] * count


def smem(count):
    return [pl.BlockSpec(memory_space=pltpu.SMEM)] * count


def circuit_of(tiles, waves):
    pairs = []
    for wave in range(0, waves, 2):
        path = [tile * waves + wave for tile in range(tiles)]
        if wave + 1 < waves:
            path += [tile * waves + wave + 1 for tile in reversed(range(tiles))]
        pairs += [(node, path[(step + 1) % len(path)]) for step, node in enumerate(path)]
    return pairs


def shards(fibre_data, kernels, block_index, live_count):
    tiles, devices = lax.axis_size("tile"), lax.axis_size("tile") * lax.axis_size("wave")
    _, groups, slots, spaxels, fibres = kernels.shape
    waves = fibre_data.shape[0]
    place = lax.axis_index("tile").reshape(1)
    lane = (lax.axis_index("wave") % 2).reshape(1)
    index = jnp.swapaxes(block_index, 1, 2).reshape(slots, groups)
    source = kernels.reshape(groups, slots, spaxels, fibres)
    turned = jax.ShapeDtypeStruct((groups, fibres, slots * spaxels), kernels.dtype)
    window = jax.ShapeDtypeStruct((EXTENT, waves, spaxels), jnp.float32)
    rim = jax.ShapeDtypeStruct((RIM * waves + SCALE_ROWS, spaxels), jnp.bfloat16)
    half_rim = jax.ShapeDtypeStruct((HALO_BLOCKS * waves + SCALE_ROWS, spaxels), jnp.bfloat16)
    moment = jax.ShapeDtypeStruct((MOMENT_ROWS, spaxels), jnp.float32)
    moment_all = jax.ShapeDtypeStruct((devices, 1, spaxels), jnp.float32)
    params = pltpu.CompilerParams(vmem_limit_bytes=VMEM_LIMIT)
    circuit = circuit_of(tiles, lax.axis_size("wave"))
    reverse = [(j, i) for i, j in circuit]

    def swap(onward, back):
        axes = ("tile", "wave")
        return lax.ppermute(onward, axes, circuit), lax.ppermute(back, axes, reverse)

    chunks = CHUNKS if groups % CHUNKS == 0 else 1
    weights, turned, held, onward, back = pl.pallas_call(
        rhs_kernel,
        out_shape=(jax.ShapeDtypeStruct(source.shape, source.dtype), turned, window, rim, rim),
        in_specs=smem(4) + [pl.BlockSpec(memory_space=pltpu.HBM)] * 2,
        out_specs=tuple(vmem(5)),
        scratch_shapes=[
            pltpu.VMEM(fibre_data.shape, fibre_data.dtype),
            pltpu.VMEM(fibre_data.shape, jnp.float32),
            pltpu.SemaphoreType.DMA((chunks,)),
            pltpu.SemaphoreType.DMA,
        ],
        compiler_params=params,
        name="rhs",
    )(
        place,
        lane,
        live_count,
        pltpu.with_memory_space_constraint(index, pltpu.HBM),
        pltpu.with_memory_space_constraint(fibre_data, pltpu.HBM),
        pltpu.with_memory_space_constraint(source, pltpu.HBM),
    )
    scratch = [
        pltpu.VMEM((EXTENT, 2 * waves, spaxels), jnp.bfloat16),
        pltpu.VMEM((groups, 2 * waves, fibres), jnp.bfloat16),
    ]
    moments = jnp.zeros(moment.shape, jnp.float32)
    vectors = []
    for power in range(3):
        final = power == 2
        onward, back = swap(onward, back)
        out_rim = half_rim if final else rim
        vector, held, onward, back, moments = pl.pallas_call(
            functools.partial(step_kernel, tiles, power, final),
            out_shape=(window, window, out_rim, out_rim, moment_all if final else moment),
            in_specs=smem(4) + vmem(6),
            out_specs=tuple(vmem(5)),
            scratch_shapes=scratch,
            compiler_params=params,
            name=f"step{power}",
        )(place, lane, live_count, index, held, onward, back, moments, weights, turned)
        vectors.append(vector)
    onward, back = swap(onward, back)
    moments = lax.all_to_all(moments, ("tile", "wave"), 0, 0)
    out = pltpu.HBM((waves, BLOCKS_DEV, spaxels), jnp.float32)
    answer, residual, steady = pl.pallas_call(
        functools.partial(final_kernel, tiles),
        out_shape=(out, out, jax.ShapeDtypeStruct((1,), jnp.int32)),
        in_specs=smem(2) + vmem(7),
        out_specs=tuple([pl.BlockSpec(memory_space=pltpu.HBM)] * 2 + smem(1)),
        scratch_shapes=[
            pltpu.VMEM((BLOCKS_DEV, waves, spaxels), jnp.float32),
            pltpu.VMEM((waves, BLOCKS_DEV, spaxels), jnp.float32),
            pltpu.VMEM((waves, BLOCKS_DEV, spaxels), jnp.float32),
            pltpu.SemaphoreType.DMA((2,)),
        ],
        compiler_params=params,
        name="combine",
    )(place, lane, moments, *vectors, held, onward, back)

    def settled(held, onward, back):
        def decoded(code):
            scale = code[RIM * waves :].astype(jnp.float32) / CODE_PEAK
            code = code[: RIM * waves].astype(jnp.float32).reshape(-1, SCALE_ROWS, spaxels)
            root = jnp.sqrt(jnp.sqrt(jnp.sqrt(jnp.abs(code))))
            return (jnp.where(code < 0.0, -root, root) * scale).reshape(RIM, waves, spaxels)

        first = lane[0] == 0
        below = decoded(jnp.where(first, onward, back))
        above = decoded(jnp.where(first, back, onward))
        held = held.at[:RIM].add(jnp.where(place[0] > 0, below, 0.0))
        return held.at[EXTENT - RIM :].add(jnp.where(place[0] < tiles - 1, above, 0.0))

    def owned(vector):
        return vector[HALO_BLOCKS : HALO_BLOCKS + BLOCKS_DEV]

    def inner(first, second):
        return lax.psum(jnp.sum(owned(first) * owned(second)), ("tile", "wave"))

    def plain(operands):
        start, _, _ = operands
        none = jnp.zeros(rim.shape, rim.dtype)

        def iterate(_, state):
            total, left, direction, norm = state
            _, held, onward, back, _ = pl.pallas_call(
                functools.partial(step_kernel, tiles, 0, False),
                out_shape=(window, window, rim, rim, moment),
                in_specs=smem(4) + vmem(6),
                out_specs=tuple(vmem(5)),
                scratch_shapes=scratch,
                compiler_params=params,
                name="plain",
            )(
                place,
                lane,
                live_count,
                index,
                direction,
                none,
                none,
                jnp.zeros(moment.shape, jnp.float32),
                source,
                jnp.swapaxes(source.reshape(groups, slots * spaxels, fibres), 1, 2),
            )
            applied = settled(held, *swap(onward, back))
            size = norm / inner(direction, applied)
            total = total + size * direction
            left = left - size * applied
            following = inner(left, left)
            direction = left + (following / norm) * direction
            return total, left, direction, following

        state = (jnp.zeros_like(start), start, start, inner(start, start))
        total, left, _, _ = lax.fori_loop(0, ITERATIONS, iterate, state)
        return jnp.swapaxes(owned(total), 0, 1), jnp.swapaxes(owned(left), 0, 1)

    def kept(operands):
        return operands[1], operands[2]

    return lax.cond(steady[0] == 1, kept, plain, (vectors[0], answer, residual))


def solution(mesh):
    in_specs = (
        P("wave", "tile", None),
        P("wave", "tile", None, None, None),
        P("wave", "tile", None),
        P("tile"),
    )
    out_specs = (P("wave", "tile", None), P("wave", "tile", None))
    return jax.shard_map(shards, mesh=mesh, in_specs=in_specs, out_specs=out_specs, check_vma=False)
```
